32 devices in a mesh: cluster: 4 (over y, core), sub: 8 (over z, x).
Axes of the slice: x: 2, y: 2, z: 4, core: 2. Of those that a mesh axis runs over, the one named last changes fastest.
Arguments:
- load: float32 [57344, 256], P(('cluster', 'sub'))
- schur: float32 [57344, 1792], P(('cluster', 'sub')), as said below
- modes: float32 [57344, 128], P(('cluster', 'sub')), may hold values from -0.125 to 0.125
- coarse_inverse: float32 [4096, 1024], P(('cluster', 'sub')), as said below
- interface_rows: int32 [32], P(('cluster', 'sub')), may hold values from 896 to 1792, as said below
- mode_count: int32 [32], P(('cluster', 'sub')), may hold values from 64 to 128, as said below
- left_rows: int32 [32, 384], P(('cluster', 'sub')), may hold values from 0 to 1792, as said below
- right_rows: int32 [32, 384], P(('cluster', 'sub')), may hold values from 0 to 1792, as said below
Outputs:
- solution: float32 [57344, 256], P(('cluster', 'sub'))
- residual: float32 [57344, 256], P(('cluster', 'sub'))
The draws below stay inside these ranges and needn't reach their ends.
Inputs may be any that keep to these rules, and one draw needn't show every extreme that they name: `interface_rows`: every subdomain has at least half of 1792 live rows, and some subdomain has exactly 1792. `mode_count`: every subdomain has at least half of 128 live modes, and some subdomain has exactly 128. Slot j of right_rows[g] and slot j of left_rows[g + 1] name the same interface unknown; the used slots of a row come first, all other slots hold 1792. Two neighbours share at least half of 384 rows and some pair shares exactly 384. The used entries of left_rows[g] and right_rows[g] are distinct live rows of g. left_rows[0] and right_rows[31] are unused. `right_rows`: see left_rows. `schur`: each block S_g is symmetric positive definite with a positive diagonal. `coarse_inverse`: each cluster's coarse inverse is symmetric positive definite.
All inputs are finite; a program needn't handle non-finite values.
Results may differ from the reference program's by a relative error of at most 0.0001.
Values sent between devices are 32-bit elements; how exact they have to be, the bound alone decides.
No kernel may reach another device: no remote copies, remote signals or barrier semaphores. Data moves between devices by JAX's collectives and lax.ppermute only.
A program may use at most 128 MiB of HBM per device.

```python
import math
import jax
import jax.numpy as jnp
from jax import lax

NI = 1792
NS = 384
K = 256
NM = 128
ITERS = 3
CLUSTERS = 4
SUBS = 32
CO = 1024


def interface_layout(key):
    base = jax.random.fold_in(key, 11)
    subkeys = jax.random.split(base, 5)
    orders = jax.random.randint(subkeys[0], (SUBS,), NI // 2, NI + 1)
    orders = orders.at[jax.random.randint(subkeys[1], (), 0, SUBS)].set(NI)
    shared = jax.random.randint(subkeys[2], (SUBS - 1,), NS // 2, NS + 1)
    shared = shared.at[jax.random.randint(subkeys[3], (), 0, SUBS - 1)].set(NS)
    nothing = jnp.zeros((1,), jnp.int32)
    right_count = jnp.concatenate([shared, nothing])
    left_count = jnp.concatenate([nothing, shared])
    scores = jax.random.randint(subkeys[4], (SUBS, NI), 0, 1048576)
    positions = jnp.arange(NI, dtype=jnp.int32)
    ranked = jnp.where(positions[None, :] < orders[:, None], scores, 1048576) * NI + positions[None, :]
    picked = jnp.argsort(ranked, axis=1, stable=True)[:, :2 * NS].astype(jnp.int32)
    slots = jnp.arange(NS, dtype=jnp.int32)
    right_index = jnp.where(slots[None, :] < right_count[:, None], picked[:, :NS], NI)
    left_index = jnp.where(slots[None, :] < left_count[:, None], picked[:, NS:], NI)
    return (orders.astype(jnp.int32), left_index.astype(jnp.int32), right_index.astype(jnp.int32))


def draw_interface_rows(key, part):
    return interface_layout(key)[0]


def draw_left_rows(key, part):
    return interface_layout(key)[1]


def draw_right_rows(key, part):
    return interface_layout(key)[2]


def draw_mode_count(key, part):
    base = jax.random.fold_in(key, 23)
    first_key, second_key = jax.random.split(base)
    counts = jax.random.randint(first_key, (SUBS,), NM // 2, NM + 1)
    counts = counts.at[jax.random.randint(second_key, (), 0, SUBS)].set(NM)
    return counts.astype(jnp.int32)


def draw_schur(key, part):
    base = jax.random.fold_in(key, 31)

    def single(index):
        sub_key = jax.random.fold_in(base, index)
        noise_key, diag_key = jax.random.split(sub_key)
        raw = jax.random.normal(noise_key, (NI, NI), jnp.float32) * (0.8 / math.sqrt(NI))
        diagonal = jax.random.uniform(diag_key, (NI,), jnp.float32, 3.0, 6.0)
        return raw + raw.T + jnp.diag(diagonal)
    return lax.map(single, jnp.arange(SUBS)).reshape(SUBS * NI, NI)


def draw_coarse_inverse(key, part):
    base = jax.random.fold_in(key, 37)

    def single(index):
        sub_key = jax.random.fold_in(base, index)
        noise_key, diag_key = jax.random.split(sub_key)
        raw = jax.random.normal(noise_key, (CO, CO), jnp.float32) * (0.25 / math.sqrt(CO))
        diagonal = jax.random.uniform(diag_key, (CO,), jnp.float32, 1.0, 2.0)
        return raw + raw.T + jnp.diag(diagonal)
    return lax.map(single, jnp.arange(CLUSTERS)).reshape(CLUSTERS * CO, CO)


def draw_load(key, part):
    base = jax.random.fold_in(key, 41)
    subkeys = jax.random.split(base, 1)
    ramp = 1.0 + 2.0 * jnp.arange(SUBS, dtype=jnp.float32) / max(SUBS - 1, 1)
    values = jax.random.normal(subkeys[0], (SUBS, NI, K), jnp.float32)
    return (values * ramp[:, None, None]).reshape(SUBS * NI, K)


def block_scale(stream_key, dims, pieces, low, top_value):
    def one(dim, shards_of):
        draws = jax.random.uniform(jax.random.fold_in(jax.random.fold_in(stream_key, 6), dim), (shards_of,), jnp.float32, low / len(pieces), top_value / len(pieces))
        return jnp.repeat(jnp.exp(draws), dims[dim] // shards_of).reshape((-1,) + (1,) * (len(dims) - dim - 1))

    level = one(*pieces[0])
    for cut in pieces[1:]:
        level = level * one(*cut)
    return level


def scatter_about(key, extent, width, most, cuts=(), held_as=jnp.bfloat16):
    entries = jax.random.normal(key, extent, jnp.float32) * width
    if len(cuts) > 0:
        entries = block_scale(key, extent, cuts, -0.22, 0.18) * entries
    return jnp.clip(entries, min=-most, max=most).astype(held_as)


def setup_inputs(seed: int = 0) -> dict:
    arg_keys = jax.random.split(jax.random.key(seed), 9)
    return {
        "load": draw_load(jax.random.fold_in(arg_keys[8], 71), 0),
        "schur": draw_schur(jax.random.fold_in(arg_keys[8], 71), 0),
        "modes": scatter_about(arg_keys[2], (SUBS * NI, NM), NI ** -0.5, 0.125, ((0, 32),), jnp.float32),
        "coarse_inverse": draw_coarse_inverse(jax.random.fold_in(arg_keys[8], 71), 0),
        "interface_rows": draw_interface_rows(jax.random.fold_in(arg_keys[8], 71), 0),
        "mode_count": draw_mode_count(jax.random.fold_in(arg_keys[8], 71), 0),
        "left_rows": draw_left_rows(jax.random.fold_in(arg_keys[8], 71), 0),
        "right_rows": draw_right_rows(jax.random.fold_in(arg_keys[8], 71), 0),
    }


def take_rows(field, indices):
    return jnp.take(field, indices, axis=0, mode="fill", fill_value=0.0)


def add_rows(field, indices, values):
    return field.at[indices].add(values, mode="drop")


def assemble(field, left_rows, right_rows):
    to_left = jax.vmap(take_rows)(field, left_rows)
    to_right = jax.vmap(take_rows)(field, right_rows)
    nothing = jnp.zeros_like(to_left[:1])
    from_left = jnp.concatenate([nothing, to_right[:-1]], 0)
    from_right = jnp.concatenate([to_left[1:], nothing], 0)
    merged = jax.vmap(add_rows)(field, left_rows, from_left)
    return jax.vmap(add_rows)(merged, right_rows, from_right)


def schur_apply(operands):
    return jnp.dot(operands[0], operands[1], precision=lax.Precision.HIGHEST, preferred_element_type=jnp.float32)


def reference(load, schur, modes, coarse_inverse, interface_rows, mode_count, left_rows, right_rows):
    highest = lax.Precision.HIGHEST
    load_blocks = load.reshape(SUBS, NI, K)
    schur_blocks = schur.reshape(SUBS, NI, NI)
    mode_blocks = modes.reshape(SUBS, NI, NM)
    coarse_blocks = coarse_inverse.reshape(CLUSTERS, CO, CO)
    positions = jnp.arange(NI, dtype=jnp.int32)
    live = (positions[None, :] < interface_rows[:, None]).astype(jnp.float32)
    ones_shared = jnp.ones((NS,), jnp.float32)

    def multiplicity(left_index, right_index):
        counted = jnp.zeros((NI,), jnp.float32).at[left_index].add(ones_shared, mode="drop")
        return counted.at[right_index].add(ones_shared, mode="drop")

    counts = jax.vmap(multiplicity)(left_rows, right_rows)
    share = live / (1.0 + counts)
    mode_live = (jnp.arange(NM, dtype=jnp.int32)[None, :] < mode_count[:, None]).astype(jnp.float32)
    schur_diag = jnp.diagonal(schur_blocks, axis1=1, axis2=2)
    rhs = assemble(live[:, :, None] * load_blocks, left_rows, right_rows)
    solution = jnp.zeros_like(rhs)
    residual = rhs
    for iteration in range(ITERS):
        modal = jnp.einsum("gim,gik->gmk", mode_blocks, share[:, :, None] * residual, precision=highest)
        modal = modal * mode_live[:, :, None]
        stacked = modal.reshape(CLUSTERS, CO, K)
        correction = jnp.einsum("cij,cjk->cik", coarse_blocks, stacked, precision=highest)
        correction = correction.reshape(SUBS, NM, K) * mode_live[:, :, None]
        prolonged = jnp.einsum("gim,gmk->gik", mode_blocks, correction, precision=highest)
        local_part = share[:, :, None] * (prolonged + residual / schur_diag[:, :, None])
        direction = assemble(local_part, left_rows, right_rows)
        product = lax.map(schur_apply, (schur_blocks, direction))
        image = assemble(live[:, :, None] * product, left_rows, right_rows)
        numerator = jnp.sum(share[:, :, None] * residual * image, axis=(0, 1))
        denominator = jnp.sum(share[:, :, None] * image * image, axis=(0, 1))
        alpha = numerator / (denominator + 1e-6)
        solution = solution + alpha[None, None, :] * direction
        residual = residual - alpha[None, None, :] * image
    return solution.reshape(SUBS * NI, K), residual.reshape(SUBS * NI, K)
```

```python
import functools

import jax
import jax.numpy as jnp
from jax import lax
from jax.experimental import pallas as pl
from jax.experimental.pallas import tpu as pltpu
from jax.sharding import PartitionSpec as P

BOTH = ("cluster", "sub")
F32 = jnp.float32
BF16 = jnp.bfloat16
ITERS = 3
INTERPRET = False


def split2(x):
    hi = x.astype(BF16)
    return hi, (x - hi.astype(F32)).astype(BF16)


def split3(x):
    hi = x.astype(BF16)
    rest = x - hi.astype(F32)
    mid = rest.astype(BF16)
    return hi, mid, (rest - mid.astype(F32)).astype(BF16)


def mm(a, b):
    return jnp.dot(a, b, preferred_element_type=F32)


def mm_nt(a, b):
    return lax.dot_general(a, b, (((1,), (1,)), ((), ())), preferred_element_type=F32)


def mm3(a, b):
    return mm(a[0], b[0]) + (mm(a[0], b[1]) + mm(a[1], b[0]))


def pick(onehot, parts):
    return sum(mm(onehot, part) for part in parts)


def accumulate(ref, value):
    first = pl.program_id(0) == 0

    @pl.when(first)
    def _():
        ref[...] = value

    @pl.when(jnp.logical_not(first))
    def _():
        ref[...] += value


def block_of(order):
    return 256 if order % 256 == 0 else order


def call(body, name, grid, ins, outs, flops, scratch=()):
    specs = [s for _, s in ins]
    arrays = [a for a, _ in ins]
    moved = sum(a.size * a.dtype.itemsize for a in arrays)
    moved += sum(functools.reduce(lambda p, q: p * q, s, 1) * jnp.dtype(d).itemsize for s, d, _ in outs)
    return pl.pallas_call(
        body,
        name=name,
        grid=grid,
        in_specs=specs,
        out_specs=[s for _, _, s in outs],
        out_shape=[jax.ShapeDtypeStruct(s, d) for s, d, _ in outs],
        scratch_shapes=list(scratch),
        cost_estimate=pl.CostEstimate(flops=int(flops), bytes_accessed=int(moved), transcendentals=0),
        compiler_params=pltpu.CompilerParams(vmem_limit_bytes=48 * 1024 * 1024),
        interpret=INTERPRET,
    )(*arrays)


def whole(a):
    shape = a.shape
    return (a, pl.BlockSpec(shape, lambda *_: (0,) * len(shape)))


def rows_of(a, b):
    return (a, pl.BlockSpec((b, a.shape[1]), lambda k: (k, 0)))


def cols_of(a, b):
    return (a, pl.BlockSpec((a.shape[0], b), lambda k: (0, k)))


def out_rows(shape, dtype, b):
    return (shape, dtype, pl.BlockSpec((b, shape[1]), lambda k: (k, 0)))


def out_cols(shape, dtype, b):
    return (shape, dtype, pl.BlockSpec((shape[0], b), lambda k: (0, k)))


def out_whole(shape, dtype):
    return (shape, dtype, pl.BlockSpec(shape, lambda *_: (0,) * len(shape)))


def scalar(a):
    return (a, pl.BlockSpec(memory_space=pltpu.SMEM))


def gather_load(index_col, load, b):
    two, (order, k) = index_col.shape[0], load.shape
    half = two // 2

    def body(idx_ref, load_ref, g_ref, left_ref, right_ref):
        lane = lax.broadcasted_iota(jnp.int32, (two, b), 1) + pl.program_id(0) * b
        onehot = jnp.where(idx_ref[...] == lane, 1.0, 0.0).astype(BF16)
        g_ref[...] = onehot
        rows = pick(onehot, split3(load_ref[...]))
        accumulate(left_ref, rows[:half])
        accumulate(right_ref, rows[half:])

    return call(
        body, "gather_load", (order // b,),
        [whole(index_col), rows_of(load, b)],
        [out_cols((two, order), BF16, b), out_whole((half, k), F32), out_whole((half, k), F32)],
        6 * two * order * k,
    )


def prepare(live_rows, live_modes, index_row, onehot, schur, modes, modes_t, b):
    two, order = onehot.shape
    half = two // 2
    nm = modes.shape[1]
    pieces = half // nm
    tall = half + 8 * pieces
    steps = order // b

    def body(rows_ref, count_ref, idx_ref, g_ref, s_ref, modes_ref, modes_t_ref,
             hi_ref, lo_ref, gt_ref, phi_ref, pth_ref, ptl_ref, vec_ref,
             left_ref, right_ref, pts_ref, sd_ref):
        k = pl.program_id(0)
        start = k * b
        hi, lo = split2(s_ref[...])
        hi_ref[...] = hi
        lo_ref[...] = lo
        row_id = lax.broadcasted_iota(jnp.int32, (b, two), 0) + start
        gt = jnp.where(idx_ref[...] == row_id, 1.0, 0.0)
        gt_ref[...] = gt.astype(BF16)
        g = g_ref[...]
        live_c = jnp.where(lax.broadcasted_iota(jnp.int32, (b, 1), 0) + start < rows_ref[0], 1.0, 0.0)
        live_r = jnp.where(lax.broadcasted_iota(jnp.int32, (1, b), 1) + start < rows_ref[0], 1.0, 0.0)
        share_c = live_c / (1.0 + jnp.sum(gt, axis=1, keepdims=True))
        share_r = live_r / (1.0 + jnp.sum(g.astype(F32), axis=0, keepdims=True))
        square = s_ref[:, pl.ds(pl.multiple_of(start, b), b)]
        eye = lax.broadcasted_iota(jnp.int32, (b, b), 0) == lax.broadcasted_iota(jnp.int32, (b, b), 1)
        square = jnp.where(eye, square, 0.0)
        sd_c = share_c / jnp.sum(square, axis=1, keepdims=True)
        sd_r = share_r / jnp.sum(square, axis=0, keepdims=True)
        lane = lax.broadcasted_iota(jnp.int32, (b, 128), 1)
        vec_ref[...] = jnp.where(lane == 0, share_c, jnp.where(lane == 1, live_c, sd_c))
        mask_r = jnp.where(lax.broadcasted_iota(jnp.int32, (1, nm), 1) < count_ref[0], 1.0, 0.0)
        mask_c = jnp.where(lax.broadcasted_iota(jnp.int32, (nm, 1), 0) < count_ref[0], 1.0, 0.0)
        phi = share_c * (modes_ref[...] * mask_r)
        phi_ref[...] = phi
        phi_t = share_r * (modes_t_ref[...] * mask_c)
        pth, ptl = split2(phi_t)
        pth_ref[...] = pth
        ptl_ref[...] = ptl
        shared = pick(g, split3(phi))
        accumulate(pts_ref, mm_nt(pth, g) + mm_nt(ptl, g))
        parts = [jnp.broadcast_to(p.astype(F32), (16, b)).astype(BF16) for p in split3(sd_r)]
        found = mm_nt(jnp.concatenate(parts, axis=0), g)
        accumulate(sd_ref, found[0:8] + found[16:24] + found[32:40])

        @pl.when(k == 0)
        def _():
            left_ref[:half] = shared[:half]
            right_ref[:half] = shared[half:]

        @pl.when(k > 0)
        def _():
            left_ref[:half] += shared[:half]
            right_ref[:half] += shared[half:]

        @pl.when(k == steps - 1)
        def _():
            for t in range(pieces):
                left_ref[half + 8 * t:half + 8 * t + 8] = sd_ref[:, t * nm:(t + 1) * nm]
                right_ref[half + 8 * t:half + 8 * t + 8] = sd_ref[:, half + t * nm:half + (t + 1) * nm]

    return call(
        body, "prepare", (steps,),
        [scalar(live_rows), scalar(live_modes), whole(index_row), cols_of(onehot, b),
         rows_of(schur, b), rows_of(modes, b), cols_of(modes_t, b)],
        [out_rows((order, order), BF16, b), out_rows((order, order), BF16, b),
         out_rows((order, two), BF16, b), out_rows((order, nm), F32, b),
         out_cols((nm, order), BF16, b), out_cols((nm, order), BF16, b),
         out_rows((order, 128), F32, b), out_whole((tall, nm), F32), out_whole((tall, nm), F32),
         out_whole((nm, two), F32)],
        2 * two * order * nm * 5,
        scratch=[pltpu.VMEM((8, two), F32)],
    )


def extend(onehot_t, phi, vec, from_prev, from_next, b):
    order, two = onehot_t.shape
    half = two // 2
    nm = phi.shape[1]
    pieces = half // nm

    def rows_at(ref):
        return jnp.concatenate([ref[half + 8 * t:half + 8 * t + 8] for t in range(pieces)], axis=1)

    def body(gt_ref, phi_ref, vec_ref, prev_ref, next_ref, hi_ref, lo_ref, w_ref):
        gt = gt_ref[...]
        total = vec_ref[:, 2:3]
        own = split2(phi_ref[...])
        hi_ref[:, :nm], lo_ref[:, :nm] = own
        for i, ref in enumerate((prev_ref, next_ref)):
            sel = gt[:, i * half:(i + 1) * half]
            hi, lo = split2(pick(sel, split2(ref[:half])))
            hi_ref[:, (i + 1) * nm:(i + 2) * nm] = hi
            lo_ref[:, (i + 1) * nm:(i + 2) * nm] = lo
            for part in split3(rows_at(ref)):
                wide = jnp.concatenate([part.astype(F32), part.astype(F32)], axis=0).astype(BF16)
                total = total + mm_nt(sel, wide)[:, 0:1]
        w_ref[...] = jnp.broadcast_to(total, (b, 128))

    return call(
        body, "extend", (order // b,),
        [rows_of(onehot_t, b), rows_of(phi, b), rows_of(vec, b), whole(from_prev), whole(from_next)],
        [out_rows((order, 3 * nm), BF16, b), out_rows((order, 3 * nm), BF16, b),
         out_rows((order, 128), F32, b)],
        2 * order * half * nm * 4,
    )


def restrict_start(phi_t, field, b):
    nm, order = phi_t[0].shape
    k = field.shape[1]

    def body(h_ref, l_ref, f_ref, o_ref):
        accumulate(o_ref, mm3((h_ref[...], l_ref[...]), split2(f_ref[...])))

    return call(
        body, "restrict_start", (order // b,),
        [cols_of(phi_t[0], b), cols_of(phi_t[1], b), rows_of(field, b)],
        [out_whole((nm, k), F32)], 6 * nm * order * k,
    )[0]


def restrict_finish(phi_ts, from_prev, from_next, own, scale=None, before=None):
    nm, two = phi_ts.shape
    half = two // 2
    k = own.shape[1]
    chained = scale is not None

    def body(p_ref, a_ref, c_ref, m_ref, *rest):
        left = mm3(split2(p_ref[:, :half]), split2(a_ref[...]))
        right = mm3(split2(p_ref[:, half:]), split2(c_ref[...]))
        total = m_ref[...] + (left + right)
        if chained:
            total = rest[1][...] - rest[0][0:1] * total
        rest[-1][...] = total

    ins = [whole(phi_ts), whole(from_prev), whole(from_next), whole(own)]
    if chained:
        ins += [whole(scale), whole(before)]
    return call(body, "restrict_finish", (1,), ins, [out_whole((nm, k), F32)], 6 * nm * two * k)[0]


def coarse(inverse, blocks):
    nm, co = inverse.shape
    k = blocks[0].shape[1]
    n = len(blocks)
    size = blocks[0].shape[0]

    def body(i_ref, *rest):
        o_ref = rest[n]
        xh, xl = rest[n + 1], rest[n + 2]
        for i in range(n):
            hi, lo = split2(rest[i][...])
            xh[i * size:(i + 1) * size] = hi
            xl[i * size:(i + 1) * size] = lo
        o_ref[...] = mm3(split2(i_ref[...]), (xh[...], xl[...]))

    return call(
        body, "coarse", (1,),
        [whole(inverse)] + [whole(x) for x in blocks],
        [out_whole((nm, k), F32)], 6 * nm * co * k,
        scratch=[pltpu.VMEM((co, k), BF16), pltpu.VMEM((co, k), BF16)],
    )[0]


def assemble_first(onehot_t, vec, w, load, from_prev, from_next, b):
    order, two = onehot_t.shape
    half = two // 2
    k = load.shape[1]

    def body(gt_ref, vec_ref, w_ref, f_ref, a_ref, c_ref, r_ref, xh_ref, xl_ref):
        gt = gt_ref[...]
        r = vec_ref[:, 1:2] * f_ref[...]
        r = r + pick(gt[:, :half], split3(a_ref[...]))
        r = r + pick(gt[:, half:], split3(c_ref[...]))
        r_ref[...] = r
        xh_ref[...], xl_ref[...] = split2(w_ref[:, 0:1] * r)

    return call(
        body, "assemble_first", (order // b,),
        [rows_of(onehot_t, b), rows_of(vec, b), rows_of(w, b), rows_of(load, b),
         whole(from_prev), whole(from_next)],
        [out_rows((order, k), F32, b), out_rows((order, k), BF16, b), out_rows((order, k), BF16, b)],
        6 * order * two * k,
    )


def assemble_image(onehot_t, vec, w, q, from_prev, from_next, resid, b, scale=None, image=None, last=False):
    order, two = onehot_t.shape
    half = two // 2
    k = q.shape[1]
    chained = scale is not None
    n_in = 9 if chained else 7

    def body(*refs):
        gt_ref, vec_ref, w_ref, q_ref, a_ref, c_ref, r_ref = refs[:7]
        outs = list(refs[n_in:])
        gt = gt_ref[...]
        new = q_ref[...]
        new = new + pick(gt[:, :half], split2(a_ref[...]))
        new = new + pick(gt[:, half:], split2(c_ref[...]))
        r = r_ref[...]
        if chained:
            s = refs[7][0:1]
            old = refs[8][...]
            new = old - s * new
            if not last:
                r = r - s * old
                outs.pop(0)[...] = r
        outs.pop(0)[...] = new
        weighted = vec_ref[:, 0:1] * new
        num = jnp.sum(weighted * r, axis=0, keepdims=True)
        den = jnp.sum(weighted * new, axis=0, keepdims=True)
        row = lax.broadcasted_iota(jnp.int32, (8, k), 0)
        accumulate(outs.pop(0), jnp.where(row == 0, num, jnp.where(row == 1, den, 0.0)))
        if not last:
            outs[0][...], outs[1][...] = split2(w_ref[:, 0:1] * new)

    ins = [rows_of(onehot_t, b), rows_of(vec, b), rows_of(w, b), rows_of(q, b),
           whole(from_prev), whole(from_next), rows_of(resid, b)]
    outs = []
    if chained:
        ins += [whole(scale), rows_of(image, b)]
        if not last:
            outs += [out_rows((order, k), F32, b)]
    outs += [out_rows((order, k), F32, b), out_whole((8, k), F32)]
    if not last:
        outs += [out_rows((order, k), BF16, b), out_rows((order, k), BF16, b)]
    return call(body, "assemble_image", (order // b,), ins, outs, 4 * order * two * k)


def schur_first(s, onehot, x, px, b):
    order = s[0].shape[0]
    two = onehot.shape[0]
    k = x[0].shape[1]
    n = px[0].shape[1]

    def body(sh_ref, sl_ref, g_ref, xh_ref, xl_ref, ph_ref, pl_ref, y_ref, ys_ref, qh_ref, ql_ref, qs_ref):
        sh, sl, g = sh_ref[...], sl_ref[...], g_ref[...]
        y = mm3((sh, sl), (xh_ref[...], xl_ref[...]))
        y_ref[...] = y
        accumulate(ys_ref, pick(g, split2(y)))
        parts = split2(mm3((sh, sl), (ph_ref[...], pl_ref[...])))
        qh_ref[...], ql_ref[...] = parts
        accumulate(qs_ref, pick(g, parts))

    return call(
        body, "schur_first", (order // b,),
        [rows_of(s[0], b), rows_of(s[1], b), cols_of(onehot, b), whole(x[0]), whole(x[1]),
         whole(px[0]), whole(px[1])],
        [out_rows((order, k), F32, b), out_whole((two, k), F32),
         out_rows((order, n), BF16, b), out_rows((order, n), BF16, b), out_whole((two, n), F32)],
        6 * order * order * (k + n) + 4 * two * order * (k + n),
    )


def schur_apply(s, onehot, x, b):
    order = s[0].shape[0]
    two = onehot.shape[0]
    k = x[0].shape[1]

    def body(sh_ref, sl_ref, g_ref, xh_ref, xl_ref, y_ref, ys_ref):
        y = mm3((sh_ref[...], sl_ref[...]), (xh_ref[...], xl_ref[...]))
        y_ref[...] = y
        accumulate(ys_ref, pick(g_ref[...], split2(y)))

    return call(
        body, "schur_apply", (order // b,),
        [rows_of(s[0], b), rows_of(s[1], b), cols_of(onehot, b), whole(x[0]), whole(x[1])],
        [out_rows((order, k), F32, b), out_whole((two, k), F32)],
        6 * order * order * k + 4 * two * order * k,
    )


def shared_image(q_shared, y_shared, stack):
    two, n = q_shared.shape
    half = two // 2
    nm, k = stack[0].shape

    def body(q_ref, y_ref, a_ref, b_ref, c_ref, left_ref, right_ref):
        total = y_ref[...]
        for i, ref in enumerate((a_ref, b_ref, c_ref)):
            total = total + mm3(split2(q_ref[:, i * nm:(i + 1) * nm]), split2(ref[...]))
        left_ref[...] = total[:half]
        right_ref[...] = total[half:]

    return call(
        body, "shared_image", (1,),
        [whole(q_shared), whole(y_shared)] + [whole(x) for x in stack],
        [out_whole((half, k), F32), out_whole((half, k), F32)], 6 * two * n * k,
    )


def local_image(q, y, vec, phi_t, stack, b, restrict):
    order, n = q[0].shape
    nm, k = stack[0].shape

    def body(qh_ref, ql_ref, y_ref, vec_ref, th_ref, tl_ref, a_ref, b_ref, c_ref, o_ref, *m_ref):
        total = y_ref[...]
        for i, ref in enumerate((a_ref, b_ref, c_ref)):
            part = slice(i * nm, (i + 1) * nm)
            total = total + mm3((qh_ref[:, part], ql_ref[:, part]), split2(ref[...]))
        total = vec_ref[:, 1:2] * total
        o_ref[...] = total
        if restrict:
            accumulate(m_ref[0], mm3((th_ref[...], tl_ref[...]), split2(total)))

    outs = [out_rows((order, k), F32, b)]
    if restrict:
        outs += [out_whole((nm, k), F32)]
    return call(
        body, "local_image", (order // b,),
        [rows_of(q[0], b), rows_of(q[1], b), rows_of(y, b), rows_of(vec, b),
         cols_of(phi_t[0], b), cols_of(phi_t[1], b)] + [whole(x) for x in stack],
        outs, 6 * order * n * k + 6 * nm * order * k,
    )


def directions(px, w, scales, resids, image, stacks, b):
    order, n = px[0].shape
    nm, k = stacks[0][0].shape
    (a0, a1), (r0, r1) = scales, resids
    c0, e0, e1 = stacks

    def body(h_ref, l_ref, w_ref, a0_ref, a1_ref, r0_ref, r1_ref, i1_ref, *rest):
        sol_ref, res_ref, dir_ref = rest[9:]
        s0, s1 = a0_ref[0:1], a1_ref[0:1]
        wc = w_ref[:, 0:1]
        x0, x1 = r0_ref[...], r1_ref[...]
        x2 = x1 - s1 * i1_ref[...]
        sol = wc * (s0 * x0 + s1 * x1)
        last = wc * x2
        for i in range(3):
            part = slice(i * nm, (i + 1) * nm)
            p = (h_ref[:, part], l_ref[:, part])
            c = rest[i][...]
            d = c - s0 * rest[3 + i][...]
            f = d - s1 * rest[6 + i][...]
            sol = sol + mm3(p, split2(s0 * c + s1 * d))
            last = last + mm3(p, split2(f))
        sol_ref[...] = sol
        res_ref[...] = x2
        dir_ref[...] = last

    return call(
        body, "directions", (order // b,),
        [rows_of(px[0], b), rows_of(px[1], b), rows_of(w, b), whole(a0), whole(a1),
         rows_of(r0, b), rows_of(r1, b), rows_of(image, b)] + [whole(x) for x in (*c0, *e0, *e1)],
        [out_rows((order, k), F32, b)] * 3, 12 * order * n * k,
    )


def passed_along(value, by):
    n = lax.axis_size(BOTH)
    return lax.ppermute(value, BOTH, [(i, i + by) for i in range(n) if 0 <= i + by < n])


def exchanged(to_prev, to_next):
    return passed_along(to_next, 1), passed_along(to_prev, -1)


def power_of_two(n):
    return n & (n - 1) == 0


def summed(value):
    for axis in BOTH:
        n = lax.axis_size(axis)
        if not power_of_two(n):
            value = lax.psum(value, axis)
            continue
        step = 1
        while step < n:
            value = value + lax.ppermute(value, axis, [(i, i ^ step) for i in range(n)])
            step *= 2
    return value


def direct(n):
    return power_of_two(n) and n <= 8


def cluster_blocks(modal):
    n = lax.axis_size("sub")
    if not direct(n):
        return [lax.all_gather(modal, "sub", axis=0, tiled=True)]
    return [modal] + [lax.ppermute(modal, "sub", [(i, i ^ d) for i in range(n)]) for d in range(1, n)]


def ordered_inverse(inverse):
    n = lax.axis_size("sub")
    if not direct(n):
        return inverse
    me = lax.axis_index("sub")
    size = inverse.shape[1] // n
    return jnp.concatenate(
        [lax.dynamic_slice_in_dim(inverse, (me ^ d) * size, size, 1) for d in range(n)], axis=1
    )


def local(load, schur, modes, coarse_inverse, interface_rows, mode_count, left_rows, right_rows):
    b = block_of(schur.shape[0])
    index_row = jnp.concatenate([left_rows, right_rows], axis=1)
    index_col = index_row.reshape(-1, 1)
    inverse = ordered_inverse(coarse_inverse)

    onehot, left, right = gather_load(index_col, load, b)
    from_prev, from_next = exchanged(left, right)
    s_hi, s_lo, onehot_t, phi, pt_hi, pt_lo, vec, phi_left, phi_right, phi_ts = prepare(
        interface_rows, mode_count, index_row, onehot, schur, modes, modes.T, b
    )
    s, phi_t = (s_hi, s_lo), (pt_hi, pt_lo)
    phi_prev, phi_next = exchanged(phi_left, phi_right)
    own = restrict_start(phi_t, load, b)
    modal = restrict_finish(phi_ts, from_prev, from_next, own)
    blocks = cluster_blocks(modal)
    px_hi, px_lo, w = extend(onehot_t, phi, vec, phi_prev, phi_next, b)
    px = (px_hi, px_lo)
    resid, x_hi, x_lo = assemble_first(onehot_t, vec, w, load, from_prev, from_next, b)
    y, y_shared, q_hi, q_lo, q_shared = schur_first(s, onehot, (x_hi, x_lo), px, b)
    q = (q_hi, q_lo)

    scales, resids, stacks = [], [resid], []
    image = scale = None
    for iteration in range(ITERS):
        last = iteration == ITERS - 1
        center = coarse(inverse, blocks)
        before, after = exchanged(center, center)
        stack = (center, before, after)
        stacks.append(stack)
        left, right = shared_image(q_shared, y_shared, stack)
        from_prev, from_next = exchanged(left, right)
        found = local_image(q, y, vec, phi_t, stack, b, not last)
        field = found[0]
        if iteration > 0:
            scale = sums[0:1] / (sums[1:2] + 1e-06)
            scale = jnp.broadcast_to(scale, (8, scale.shape[1]))
            scales.append(scale)
        if not last:
            previous = modal
            modal = restrict_finish(phi_ts, from_prev, from_next, found[1], scale,
                                    None if scale is None else image_modal)
            image_modal = modal
            blocks = cluster_blocks(modal)
            made = assemble_image(onehot_t, vec, w, field, from_prev, from_next, resid, b, scale, image)
            if iteration > 0:
                resid, made = made[0], made[1:]
                resids.append(resid)
            image, sums, x_hi, x_lo = made
            sums = summed(sums)
            y, y_shared = schur_apply(s, onehot, (x_hi, x_lo), b)
        else:
            sol, resid, final = directions(px, w, scales, resids, image, stacks, b)
            image, sums = assemble_image(onehot_t, vec, w, field, from_prev, from_next, resid, b,
                                         scale, image, last=True)
            sums = summed(sums)
    scale = sums[0:1] / (sums[1:2] + 1e-06)
    return sol + scale * final, resid - scale * image


def solution(mesh):
    rows = P(BOTH, None)
    return jax.shard_map(
        local,
        mesh=mesh,
        in_specs=(rows, rows, rows, rows, P(BOTH), P(BOTH), rows, rows),
        out_specs=(rows, rows),
        check_vma=False,
    )
```

```python
import jax
import jax.numpy as jnp
from jax import lax
from jax.experimental import pallas as pl
from jax.experimental.pallas import tpu as pltpu
from jax.sharding import PartitionSpec as P

BOTH = ("cluster", "sub")
F32 = jnp.float32
BF16 = jnp.bfloat16
ITERS = 3
INTERPRET = False
SUMS = 8


def split2(x):
    hi = x.astype(BF16)
    return hi, (x - hi.astype(F32)).astype(BF16)


def split3(x):
    hi = x.astype(BF16)
    rest = x - hi.astype(F32)
    mid = rest.astype(BF16)
    return hi, mid, (rest - mid.astype(F32)).astype(BF16)


def mm(a, b):
    return jnp.dot(a, b, preferred_element_type=F32)


def mm3(a, b):
    return mm(jnp.concatenate([a[0], a[0]], 1), jnp.concatenate([b[0], b[1]], 0)) + mm(a[1], b[0])


def pick(onehot, parts):
    return mm(jnp.concatenate([onehot] * len(parts), 1), jnp.concatenate(parts, 0))


def shape(*dims, dtype=F32):
    return jax.ShapeDtypeStruct(dims, dtype)


def call(body, name, ins, outs, flops, scalars=(), scratch=(), mb=8):
    moved = sum(a.size * a.dtype.itemsize for a in (*ins, *outs))
    found = pl.pallas_call(
        body,
        name=name,
        in_specs=[pl.BlockSpec(memory_space=pltpu.SMEM)] * len(scalars)
        + [pl.BlockSpec(memory_space=pltpu.VMEM)] * len(ins),
        out_specs=[pl.BlockSpec(memory_space=pltpu.VMEM)] * len(outs),
        out_shape=list(outs),
        scratch_shapes=list(scratch),
        cost_estimate=pl.CostEstimate(flops=int(flops), bytes_accessed=int(moved), transcendentals=0),
        compiler_params=pltpu.CompilerParams(vmem_limit_bytes=mb * 1024 * 1024),
        interpret=INTERPRET,
    )(*scalars, *ins)
    return found


def over_blocks(order, step, carry=0, unroll=False):
    b = block_of(order)
    if unroll:
        for k in range(0, order, b):
            carry = step(pl.ds(k, b), k, carry)
        return carry

    def one(k, carry):
        at = pl.multiple_of(k * b, b)
        return step(pl.ds(at, b), at, carry)

    return lax.fori_loop(0, order // b, one, carry)


def block_of(order):
    return 256 if order % 256 == 0 else order


def gather_rows(source, index, outs, half, order):
    group = 8 if half % 8 == 0 else 1
    for side, out in enumerate(outs):

        def step(j, _, side=side, out=out):
            for u in range(group):
                slot = j * group + u
                row = jnp.minimum(index(side, slot), order - 1)
                out[pl.ds(slot, 1), :] = source[pl.ds(row, 1), :]
            return 0

        lax.fori_loop(0, half // group, step, 0)


def sides(me_ref, left_ref, right_ref):
    even = lax.rem(me_ref[0], 2) == 0

    def index(side, slot):
        a, c = (right_ref, left_ref) if side == 0 else (left_ref, right_ref)
        return jnp.where(even, a[0, slot], c[0, slot])

    return index


def row_sides(me_ref, left_ref, right_ref):
    even = lax.rem(me_ref[0], 2) == 0
    left, right = left_ref[...], right_ref[...]
    return jnp.where(even, right, left), jnp.where(even, left, right)


def used_slots(out, count):
    slot = lax.broadcasted_iota(jnp.int32, out.shape, 0)
    out[...] = jnp.where(slot < count, out[...], 0.0)


def used_count(row, order):
    return jnp.sum(jnp.where(row < order, 1, 0))


def gather_load(me, left, right, load):
    half = left.shape[1]
    order, k = load.shape

    def body(me_ref, ls_ref, rs_ref, lv_ref, rv_ref, load_ref, x_ref, d_ref):
        gather_rows(load_ref, sides(me_ref, ls_ref, rs_ref), (x_ref, d_ref), half, order)
        rows = row_sides(me_ref, lv_ref, rv_ref)
        used_slots(x_ref, used_count(rows[0], order))
        used_slots(d_ref, used_count(rows[1], order))

    return call(body, "gather_load", [left, right, load], [shape(half, k)] * 2, 0, [me, left, right])


def halves(me, inverse):
    nm, co = inverse.shape

    def body(me_ref, c_ref, same_ref, other_ref):
        par = lax.rem(me_ref[0], 2)
        for j in range(co // nm // 2):
            to = slice(j * nm, (j + 1) * nm)
            same_ref[:, to] = c_ref[:, pl.ds(pl.multiple_of((2 * j + par) * nm, nm), nm)]
            other_ref[:, to] = c_ref[:, pl.ds(pl.multiple_of((2 * j + 1 - par) * nm, nm), nm)]

    return call(body, "halves", [inverse], [shape(nm, co // 2)] * 2, 0, [me])


def prepare(me, live_rows, live_modes, left, right, schur, modes):
    order, nm = modes.shape
    half = left.shape[1]
    two = 2 * half
    pieces = half // nm
    tall = half + 8 * pieces
    b = block_of(order)

    def body(me_ref, rows_ref, count_ref, l_ref, r_ref, s_ref, modes_ref,
             gt_ref, ph_ref, pl_ref, pth_ref, ptl_ref, vec_ref, x_ref, d_ref, tsh_ref, tsl_ref):
        index = jnp.concatenate(row_sides(me_ref, l_ref, r_ref), axis=1)
        mask = jnp.where(lax.broadcasted_iota(jnp.int32, (1, nm), 1) < count_ref[0], 1.0, 0.0)
        eye = lax.broadcasted_iota(jnp.int32, (b, b), 0) == lax.broadcasted_iota(jnp.int32, (b, b), 1)
        lane = lax.broadcasted_iota(jnp.int32, (b, 128), 1)

        def step(r, start, carry):
            shared, weights = carry
            row_id = lax.broadcasted_iota(jnp.int32, (b, two), 0) + start
            found = jnp.where(index == row_id, 1.0, 0.0)
            gt = found.astype(BF16)
            gt_ref[r] = gt
            live = jnp.where(lax.broadcasted_iota(jnp.int32, (b, 1), 0) + start < rows_ref[0], 1.0, 0.0)
            share = live / (1.0 + jnp.sum(found, axis=1, keepdims=True))
            diag = jnp.sum(jnp.where(eye, s_ref[r, r], 0.0), axis=1, keepdims=True)
            sd = share / diag
            weights = weights + jnp.sum(found * sd, axis=0, keepdims=True)
            vec_ref[r] = jnp.where(lane == 0, live, sd)
            phi = share * (modes_ref[r] * mask)
            ph_ref[r], pl_ref[r] = split2(phi)
            parts = split3(phi.T)
            pth_ref[:, r], ptl_ref[:, r] = split2(phi.T)
            return shared + mm(jnp.concatenate(parts, 1), jnp.concatenate([gt] * 3, 0)), weights

        shared, weights = over_blocks(
            order, step, (jnp.zeros((nm, two), F32), jnp.zeros((1, two), F32))
        )
        tsh_ref[...], tsl_ref[...] = split2(shared)
        back = shared.T
        for i, ref in enumerate((x_ref, d_ref)):
            ref[:half] = back[i * half:(i + 1) * half]
            for t in range(pieces):
                at = i * half + t * nm
                ref[half + 8 * t:half + 8 * t + 8] = jnp.broadcast_to(weights[:, at:at + nm], (8, nm))

    half_type = dict(dtype=BF16)
    return call(
        body, "prepare", [left, right, schur, modes],
        [shape(order, two, **half_type), shape(order, nm, **half_type), shape(order, nm, **half_type),
         shape(nm, order, **half_type), shape(nm, order, **half_type), shape(order, 128),
         shape(tall, nm), shape(tall, nm), shape(nm, two, **half_type), shape(nm, two, **half_type)],
        6 * two * order * nm, [me, live_rows, live_modes], mb=10,
    )


def start(schur, phi, phi_t, load):
    order, nm = phi[0].shape
    k = load.shape[1]

    def body(s_ref, h_ref, l_ref, th_ref, tl_ref, f_ref, q_ref, m_ref):
        m_ref[...] = mm3((th_ref[...], tl_ref[...]), split2(f_ref[...]))

        def step(r, _, carry):
            q_ref[r] = mm3(split2(s_ref[r]), (h_ref[...], l_ref[...]))
            return carry

        over_blocks(order, step)

    return call(
        body, "start", [schur, *phi, *phi_t, load], [shape(order, nm), shape(nm, k)],
        6 * order * order * nm + 6 * nm * order * k, mb=12,
    )


def extend(onehot_t, vec, load, recv, phi_recv):
    order, two = onehot_t.shape
    half = two // 2
    k = load.shape[1]
    nm = phi_recv[0].shape[1]
    pieces = half // nm

    def body(gt_ref, vec_ref, f_ref, rx_ref, rd_ref, px_ref, pd_ref, r_ref, w_ref, xh_ref, xl_ref, nh_ref, nl_ref):
        field = [jnp.concatenate(p, 0) for p in zip(split3(rx_ref[...]), split3(rd_ref[...]))]
        weights = jnp.concatenate(
            [ref[half + 8 * t:half + 8 * t + 1] for ref in (px_ref, pd_ref) for t in range(pieces)], axis=1
        )
        modes = [jnp.concatenate(split2(ref[:half]), 0) for ref in (px_ref, pd_ref)]

        def step(r, _, carry):
            gt = gt_ref[r]
            w = vec_ref[r, 1:2] + jnp.sum(gt.astype(F32) * weights, axis=1, keepdims=True)
            w_ref[r] = jnp.broadcast_to(w, (w.shape[0], 128))
            rhs = vec_ref[r, 0:1] * f_ref[r] + pick(gt, field)
            r_ref[r] = rhs
            xh_ref[r], xl_ref[r] = split2(w * rhs)
            for i in range(2):
                side = gt[:, i * half:(i + 1) * half]
                part = mm(jnp.concatenate([side, side], 1), modes[i])
                nh_ref[r, i * nm:(i + 1) * nm], nl_ref[r, i * nm:(i + 1) * nm] = split2(part)
            return carry

        over_blocks(order, step)

    return call(
        body, "extend", [onehot_t, vec, load, *recv, *phi_recv],
        [shape(order, k), shape(order, 128)] + [shape(order, k, dtype=BF16)] * 2
        + [shape(order, 2 * nm, dtype=BF16)] * 2,
        2 * order * two * (3 * k + 2 * nm), mb=12,
    )


def schur_first(me, left, right, schur, x, phi_n, q_own):
    order, k = x[0].shape
    half = left.shape[1]
    nm = q_own.shape[1]
    n = 3 * nm

    def body(me_ref, ls_ref, rs_ref, s_ref, xh_ref, xl_ref, nh_ref, nl_ref, qo_ref, y_ref, ys_ref, q_ref, qs_ref):
        rhs = (jnp.concatenate([xh_ref[...], nh_ref[...]], 1), jnp.concatenate([xl_ref[...], nl_ref[...]], 1))

        def block(r, _, carry):
            both = mm3(split2(s_ref[r]), rhs)
            y_ref[r] = both[:, :k]
            q_ref[r, nm:] = both[:, k:]
            q_ref[r, :nm] = qo_ref[r]
            return carry

        over_blocks(order, block, unroll=True)
        index = sides(me_ref, ls_ref, rs_ref)
        group = 8 if half % 8 == 0 else 1
        for side in range(2):

            def step(j, _, side=side):
                for u in range(group):
                    slot = j * group + u
                    row = jnp.minimum(index(side, slot), order - 1)
                    ys_ref[pl.ds(side * half + slot, 1), :] = y_ref[pl.ds(row, 1), :]
                    qs_ref[pl.ds(side * half + slot, 1), :] = q_ref[pl.ds(row, 1), :]
                return 0

            lax.fori_loop(0, half // group, step, 0)

    return call(
        body, "schur_first", [schur, *x, *phi_n, q_own],
        [shape(order, k), shape(2 * half, k), shape(order, n), shape(2 * half, n)],
        6 * order * order * (k + 2 * nm), [me, left, right], mb=14,
    )


def schur_apply(me, left, right, schur, x):
    order, k = x[0].shape
    half = left.shape[1]

    def body(me_ref, ls_ref, rs_ref, s_ref, xh_ref, xl_ref, y_ref, ys_ref):
        x = (xh_ref[...], xl_ref[...])

        def block(r, _, carry):
            y_ref[r] = mm3(split2(s_ref[r]), x)
            return carry

        over_blocks(order, block, unroll=True)
        gather_rows(y_ref, sides(me_ref, ls_ref, rs_ref), (ys_ref.at[:half], ys_ref.at[half:]), half, order)

    return call(
        body, "schur_apply", [schur, *x], [shape(order, k), shape(2 * half, k)],
        6 * order * order * k, [me, left, right], mb=12,
    )


def coarse(me, inverses, modal):
    nm, co = inverses[0].shape
    rows, k = modal[0].shape
    n = len(modal)
    ordered = direct(2 * n)

    def body(me_ref, own_ref, x_ref, d_ref, z_ref, *rest):
        send_ref, keep_ref, xh, xl = rest[n:]
        pos = me_ref[0] // 2
        sums = jnp.zeros((SUMS, k), F32)
        for d in range(n):
            at = pl.ds(pl.multiple_of(((pos ^ d) if ordered else d) * nm, nm), nm)
            xh[at], xl[at] = split2(rest[d][:nm])
            sums = sums + rest[d][nm:]
        a = split2(jnp.concatenate([own_ref[...], x_ref[...], d_ref[...], z_ref[...]], 0))
        part = mm3(a, (xh[...], xl[...]))
        keep_ref[:3 * nm] = part[:3 * nm]
        keep_ref[3 * nm:] = sums
        send_ref[:nm] = part[nm:2 * nm]
        send_ref[nm:2 * nm] = part[:nm]
        send_ref[2 * nm:3 * nm] = part[3 * nm:]
        send_ref[3 * nm:] = sums

    return call(
        body, "coarse", [*inverses, *modal], [shape(3 * nm + SUMS, k)] * 2,
        24 * nm * co * k, [me], scratch=[pltpu.VMEM((co, k), BF16)] * 2, mb=12,
    )


def shared_image(me, last_sub, left, right, order, q_shared, y_shared, keep, recv, edge):
    two, n = q_shared.shape
    half = two // 2
    nm, k = edge.shape

    def body(me_ref, lv_ref, rv_ref, q_ref, y_ref, keep_ref, recv_ref, edge_ref, x_ref, d_ref, st_ref):
        rows = row_sides(me_ref, lv_ref, rv_ref)
        at_edge = jnp.logical_or(me_ref[0] == 0, me_ref[0] == last_sub)
        total = keep_ref[:3 * nm] + recv_ref[:3 * nm]
        st_ref[:2 * nm] = total[:2 * nm]
        st_ref[2 * nm:] = jnp.where(at_edge, edge_ref[...], total[2 * nm:])
        c = split2(st_ref[...])
        for i, ref in enumerate((x_ref, d_ref)):
            at = slice(i * half, (i + 1) * half)
            found = y_ref[at] + mm3(split2(q_ref[at]), c)
            slot = lax.broadcasted_iota(jnp.int32, (half, k), 0)
            ref[...] = jnp.where(slot < used_count(rows[i], order), found, 0.0)

    return call(
        body, "shared_image", [left, right, q_shared, y_shared, keep, recv, edge],
        [shape(half, k)] * 2 + [shape(3 * nm, k)], 6 * two * n * k, [me], mb=10,
    )


def local_image(q, y, vec, phi_t, stack, chain, restrict):
    order, n = q.shape
    k = stack.shape[1]
    nm = phi_t[0].shape[0]
    chained = len(chain) == 4

    def body(q_ref, y_ref, vec_ref, th_ref, tl_ref, st_ref, *refs):
        ins, outs = refs[:len(chain)], list(refs[len(chain):])
        c = split2(st_ref[...])
        p_ref = outs.pop(0)
        r_ref = outs.pop(0) if chained else None

        def step(at, _, carry):
            num, den, modal = carry
            p = vec_ref[at, 0:1] * (y_ref[at] + mm3(split2(q_ref[at]), c))
            r = ins[0][at]
            if chained:
                scale = ins[1][0:1]
                p = ins[2][at] - scale * p
                r = r - scale * ins[3][at]
                r_ref[at] = r
            p_ref[at] = p
            num = num + jnp.sum(r * p, axis=0, keepdims=True)
            den = den + jnp.sum(p * p, axis=0, keepdims=True)
            if restrict:
                modal = modal + mm3((th_ref[:, at], tl_ref[:, at]), split2(p))
            return num, den, modal

        zero = jnp.zeros((1, k), F32)
        num, den, modal = over_blocks(order, step, (zero, zero, jnp.zeros((nm, k), F32)))
        row = lax.broadcasted_iota(jnp.int32, (SUMS, k), 0)
        m_ref = outs.pop(0)
        m_ref[:nm] = modal
        m_ref[nm:] = jnp.where(row == 0, num, jnp.where(row == 1, den, 0.0))

    outs = [shape(order, k)] + ([shape(order, k)] if chained else []) + [shape(nm + SUMS, k)]
    return call(
        body, "local_image", [q, y, vec, *phi_t, stack, *chain], outs,
        6 * order * n * k + 6 * nm * order * k, mb=12,
    )


def finish(phi_ts, own, recv, sent=(), chain=()):
    nm, two = phi_ts[0].shape
    half = two // 2
    k = own.shape[1]
    plain = len(sent) == 0

    def body(h_ref, l_ref, m_ref, *refs):
        ins, outs = refs[:2 + len(sent) + len(chain)], refs[2 + len(sent) + len(chain):]
        got = jnp.concatenate([ins[0][...], ins[1][...]], 0)
        cross = jnp.zeros((1, k), F32)
        if not plain:
            put = jnp.concatenate([ins[2][...], ins[3][...]], 0)
            if chain:
                scale = ins[4][0:1]
                got = ins[5][...] - scale * got
                put = ins[6][...] - scale * put
            outs[1][...] = got
            outs[2][...] = put
            cross = jnp.sum(got * put, axis=0, keepdims=True)
        outs[0][:nm] = m_ref[:nm] + mm3((h_ref[...], l_ref[...]), split2(got))
        row = lax.broadcasted_iota(jnp.int32, (SUMS, k), 0)
        base = m_ref[nm:] if not plain else jnp.zeros((SUMS, k), F32)
        outs[0][nm:] = base + jnp.where(row == 1, cross, 0.0)

    outs = [shape(nm + SUMS, k)] + ([] if plain else [shape(two, k)] * 2)
    return call(body, "finish", [*phi_ts, own, *recv, *sent, *chain], outs, 6 * nm * two * k, mb=10)


def assemble(onehot_t, p, got, w=None):
    order, two = onehot_t.shape
    k = p.shape[1]

    def body(gt_ref, p_ref, g_ref, *refs):
        parts = jnp.concatenate(split2(g_ref[...]), 0)

        def step(r, _, carry):
            gt = gt_ref[r]
            new = p_ref[r] + mm(jnp.concatenate([gt, gt], 1), parts)
            if w is None:
                refs[0][r] = new
            else:
                w_ref, i_ref, xh_ref, xl_ref = refs
                i_ref[r] = new
                xh_ref[r], xl_ref[r] = split2(w_ref[r, 0:1] * new)
            return carry

        over_blocks(order, step)

    ins = [onehot_t, p, got] + ([] if w is None else [w])
    outs = [shape(order, k)] + ([] if w is None else [shape(order, k, dtype=BF16)] * 2)
    return call(body, "assemble", ins, outs, 4 * order * two * k, mb=10)


def directions(phi, phi_n, w, scales, resids, stacks):
    order, nm = phi[0].shape
    n, k = stacks[0].shape

    def body(h_ref, l_ref, nh_ref, nl_ref, w_ref, a0_ref, a1_ref, r0_ref, r1_ref, r2_ref,
             c0_ref, e0_ref, e1_ref, sol_ref, dir_ref):
        s0, s1 = a0_ref[0:1], a1_ref[0:1]
        c0 = c0_ref[...]
        c1 = c0 - s0 * e0_ref[...]
        first = s0 * c0 + s1 * c1
        c = split2(jnp.concatenate([first, c1 - s1 * e1_ref[...]], 1))

        def step(r, _, carry):
            p = (jnp.concatenate([h_ref[r], nh_ref[r]], 1), jnp.concatenate([l_ref[r], nl_ref[r]], 1))
            both = mm3(p, c)
            wc = w_ref[r, 0:1]
            sol_ref[r] = both[:, :k] + wc * (s0 * r0_ref[r] + s1 * r1_ref[r])
            dir_ref[r] = both[:, k:] + wc * r2_ref[r]
            return carry

        over_blocks(order, step)

    return call(
        body, "directions", [*phi, *phi_n, w, *scales, *resids, *stacks], [shape(order, k)] * 2,
        12 * order * n * k, mb=12,
    )


def swap_x(value):
    n = lax.axis_size("sub")
    return lax.ppermute(value, "sub", [(i, i ^ 1) for i in range(n)])


def swap_d(value):
    n = lax.axis_size(BOTH)
    pairs = [(i, i + 1) for i in range(1, n - 1, 2)]
    return lax.ppermute(value, BOTH, pairs + [(b, a) for a, b in pairs])


def coarse_rows(me, inverse):
    n = lax.axis_size("sub")
    same, other = halves(me, inverse)
    ring = [((i + 1) % n, (i + 2) % n) for i in range(0, n, 2)]
    at_d = lax.ppermute(other, "sub", ring + [(b, a) for a, b in ring])
    at_x = swap_x(other)
    at_z = lax.ppermute(same, "sub", [(i, (i - 2) % n if i % 2 == 0 else (i + 2) % n) for i in range(n)])
    return same, at_x, at_d, at_z


def direct(n):
    return n & (n - 1) == 0 and n <= 8


def parity_blocks(modal):
    n = lax.axis_size("sub")
    if not direct(n):
        groups = [list(range(p, n, 2)) for p in range(2)]
        every = lax.all_gather(modal, "sub", axis=0, axis_index_groups=groups)
        return [every[d] for d in range(n // 2)]
    return [modal] + [
        lax.ppermute(modal, "sub", [(i, i ^ (2 * d)) for i in range(n)]) for d in range(1, n // 2)
    ]


def over_axis(value, axis):
    n = lax.axis_size(axis)
    if n & (n - 1):
        return lax.psum(value, axis)
    step = 1
    while step < n:
        value = value + lax.ppermute(value, axis, [(i, i ^ step) for i in range(n)])
        step *= 2
    return value


def edge_blocks(block):
    n, m = lax.axis_size("sub"), lax.axis_size("cluster")
    up = [(n * c, n * (c + 1)) for c in range(m - 1)]
    down = [(n * (c + 1) + n - 1, n * c + n - 1) for c in range(m - 1)]
    return lax.ppermute(block, BOTH, up + down)


def scale_of(sums):
    value = sums[0:1] / (sums[1:2] + 1e-06)
    return jnp.broadcast_to(value, (8, value.shape[1]))


def local(load, schur, modes, coarse_inverse, interface_rows, mode_count, left_rows, right_rows):
    nm = modes.shape[1]
    n_sub = lax.axis_size("sub")
    me = lax.axis_index("sub").astype(jnp.int32).reshape(1)

    to_x, to_d = gather_load(me, left_rows, right_rows, load)
    recv = swap_x(to_x), swap_d(to_d)
    onehot_t, p_hi, p_lo, pt_hi, pt_lo, vec, phi_x, phi_d, ts_hi, ts_lo = prepare(
        me, interface_rows, mode_count, left_rows, right_rows, schur, modes
    )
    phi, phi_t, phi_ts = (p_hi, p_lo), (pt_hi, pt_lo), (ts_hi, ts_lo)
    phi_recv = swap_x(phi_x), swap_d(phi_d)
    inverses = coarse_rows(me, coarse_inverse)
    q_own, own = start(schur, phi, phi_t, load)
    own = jnp.concatenate([own, jnp.zeros((SUMS, own.shape[1]), F32)], 0)
    (modal,) = finish(phi_ts, own, recv)
    blocks = parity_blocks(modal)
    resid, w, x_hi, x_lo, n_hi, n_lo = extend(onehot_t, vec, load, recv, phi_recv)
    phi_n = (n_hi, n_lo)
    y, y_shared, q, q_shared = schur_first(me, left_rows, right_rows, schur, (x_hi, x_lo), phi_n, q_own)

    scales, resids, stacks = [], [resid], []
    for iteration in range(ITERS):
        last = iteration == ITERS - 1
        send, keep = coarse(me, inverses, blocks)
        got = swap_x(send)
        edge = edge_blocks(keep[2 * nm:3 * nm] + got[2 * nm:3 * nm])
        to_x, to_d, stack = shared_image(
            me, n_sub - 1, left_rows, right_rows, schur.shape[0], q_shared, y_shared, keep, got, edge
        )
        stacks.append(stack)
        recv = swap_x(to_x), swap_d(to_d)
        if iteration == 0:
            p, own = local_image(q, y, vec, phi_t, stack, (resid,), True)
            modal, far, near = finish(phi_ts, own, recv, (to_x, to_d))
        else:
            scale = scale_of(over_axis(keep[3 * nm:] + got[3 * nm:], "cluster"))
            scales.append(scale)
            p, resid, own = local_image(q, y, vec, phi_t, stack, (resid, scale, p, image), not last)
            resids.append(resid)
            modal, far, near = finish(phi_ts, own, recv, (to_x, to_d), (scale, far, near))
        if not last:
            blocks = parity_blocks(modal)
            image, x_hi, x_lo = assemble(onehot_t, p, far, w)
            y, y_shared = schur_apply(me, left_rows, right_rows, schur, (x_hi, x_lo))
    sums = over_axis(over_axis(modal[nm:], "cluster"), "sub")
    sol, final = directions(phi, phi_n, w, scales, resids, stacks)
    (image,) = assemble(onehot_t, p, far)
    scale = scale_of(sums)[0:1]
    return sol + scale * final, resid - scale * image


def solution(mesh):
    rows = P(BOTH, None)
    return jax.shard_map(
        local,
        mesh=mesh,
        in_specs=(rows, rows, rows, rows, P(BOTH), P(BOTH), rows, rows),
        out_specs=(rows, rows),
        check_vma=False,
    )
```

```python
import jax
import jax.numpy as jnp
from jax import lax
from jax.experimental import pallas as pl
from jax.experimental.pallas import tpu as pltpu
from jax.sharding import PartitionSpec as P


BOTH = ("cluster", "sub")
F32 = jnp.float32
BF16 = jnp.bfloat16
ITERS = 3
INTERPRET = False
SUMS = 8


def split2(x):
    hi = x.astype(BF16)
    return hi, (x - hi.astype(F32)).astype(BF16)


def split3(x):
    hi = x.astype(BF16)
    rest = x - hi.astype(F32)
    mid = rest.astype(BF16)
    return hi, mid, (rest - mid.astype(F32)).astype(BF16)


def mm(a, b):
    return jnp.dot(a, b, preferred_element_type=F32)


def mm3(a, b):
    return mm(jnp.concatenate([a[0], a[0]], 1), jnp.concatenate([b[0], b[1]], 0)) + mm(a[1], b[0])


def pick(onehot, parts):
    return mm(jnp.concatenate([onehot] * len(parts), 1), jnp.concatenate(parts, 0))


def shape(*dims, dtype=F32):
    return jax.ShapeDtypeStruct(dims, dtype)


def call(body, ins, outs, flops, scalars=(), scratch=(), mb=8, raw=(), after=()):
    moved = sum(a.size * a.dtype.itemsize for a in (*ins, *outs))
    lead = len(scalars) + len(raw) + len(ins)

    def run(*refs):
        body(*refs[:lead], *refs[lead + len(after):])

    anywhere = pl.BlockSpec(memory_space=pl.ANY)
    outside = pl.BlockSpec(memory_space=pltpu.HBM)
    on_chip = pl.BlockSpec(memory_space=pltpu.VMEM)
    return pl.pallas_call(
        run,
        in_specs=[pl.BlockSpec(memory_space=pltpu.SMEM)] * len(scalars) + [outside] * len(raw)
        + [on_chip] * len(ins) + [anywhere] * len(after),
        out_specs=[on_chip] * len(outs),
        out_shape=list(outs),
        scratch_shapes=list(scratch),
        cost_estimate=pl.CostEstimate(flops=int(flops), bytes_accessed=int(moved), transcendentals=0),
        compiler_params=pltpu.CompilerParams(vmem_limit_bytes=mb * 1024 * 1024),
        interpret=INTERPRET,
    )(*scalars, *[pltpu.with_memory_space_constraint(a, pltpu.HBM) for a in raw], *ins, *after)


def over_blocks(order, step, carry=0, unroll=False):
    b = block_of(order)
    if unroll:
        for k in range(0, order, b):
            carry = step(pl.ds(k, b), k, carry)
        return carry

    def one(k, carry):
        at = pl.multiple_of(k * b, b)
        return step(pl.ds(at, b), at, carry)

    return lax.fori_loop(0, order // b, one, carry)


def block_of(order):
    return 256 if order % 256 == 0 else order


def copy_rows(pairs, index_ref, base, half, order, masked):
    group = 8 if half % 8 == 0 else 1

    def step(j, _):
        for u in range(group):
            slot = j * group + u
            row = index_ref[0, slot]
            at = jnp.minimum(row, order - 1)
            for source, out in pairs:
                value = source[pl.ds(at, 1), :]
                out[pl.ds(base + slot, 1), :] = jnp.where(row < order, value, 0.0) if masked else value
        return 0

    lax.fori_loop(0, half // group, step, 0)


def by_parity(me, work):
    even = lax.rem(me, 2) == 0
    pl.when(even)(lambda: work(1, 0))
    pl.when(jnp.logical_not(even))(lambda: work(0, 1))


def row_sides(me_ref, left_ref, right_ref):
    even = lax.rem(me_ref[0], 2) == 0
    left, right = left_ref[...], right_ref[...]
    return jnp.where(even, right, left), jnp.where(even, left, right)


def used_count(row, order):
    return jnp.sum(jnp.where(row < order, 1, 0))


def gather_load(me, left, right, load):
    half = left.shape[1]
    order, k = load.shape

    def body(me_ref, l_hbm, r_hbm, load_hbm, x_ref, d_ref, l_ref, r_ref, load_ref, sems):
        moves = [
            pltpu.make_async_copy(source, target, sems.at[i])
            for i, (source, target) in enumerate(((l_hbm, l_ref), (r_hbm, r_ref), (load_hbm, load_ref)))
        ]
        for move in moves:
            move.start()
        for move in moves:
            move.wait()
        rows = (l_ref, r_ref)

        def work(first, second):
            copy_rows([(load_ref, x_ref)], rows[first], 0, half, order, True)
            copy_rows([(load_ref, d_ref)], rows[second], 0, half, order, True)

        by_parity(me_ref[0], work)

    return call(
        body, [], [shape(half, k)] * 2, 0, [me], raw=[left, right, load],
        scratch=[pltpu.SMEM((1, half), jnp.int32)] * 2 + [pltpu.VMEM((order, k), F32), pltpu.SemaphoreType.DMA((3,))],
    )


def gather_shared(me, left, right, fields, masked=False):
    half = left.shape[1]
    order = fields[0].shape[0]
    n = len(fields)

    def body(me_ref, l_ref, r_ref, *refs):
        rows = (l_ref, r_ref)

        def work(first, second):
            for side, index in enumerate((first, second)):
                outs = refs[n + side::2] if masked else refs[n:]
                pairs = list(zip(refs[:n], outs))
                copy_rows(pairs, rows[index], 0 if masked else side * half, half, order, masked)

        by_parity(me_ref[0], work)

    if masked:
        outs = [shape(half, f.shape[1]) for f in fields for _ in range(2)]
    else:
        outs = [shape(2 * half, f.shape[1]) for f in fields]
    return call(body, fields, outs, 2e9, [me, left, right], mb=4)


def halves(me, inverse, after):
    nm, co = inverse.shape

    def body(me_ref, c_ref, same_ref, other_ref):
        par = lax.rem(me_ref[0], 2)
        for j in range(co // nm // 2):
            to = slice(j * nm, (j + 1) * nm)
            same_ref[:, to] = c_ref[:, pl.ds(pl.multiple_of((2 * j + par) * nm, nm), nm)]
            other_ref[:, to] = c_ref[:, pl.ds(pl.multiple_of((2 * j + 1 - par) * nm, nm), nm)]

    return call(body, [inverse], [shape(nm, co // 2)] * 2, 0, [me], after=after)


def prepare(me, live_rows, live_modes, left, right, schur, modes, load):
    order, nm = modes.shape
    half = left.shape[1]
    two = 2 * half
    pieces = half // nm
    tall = half + 8 * pieces
    b = block_of(order)
    k_load = load.shape[1]

    def body(me_ref, rows_ref, count_ref, s_hbm, modes_hbm, load_hbm, l_ref, r_ref,
             gt_ref, ph_ref, pl_ref, pth_ref, ptl_ref, vec_ref, x_ref, d_ref, tsh_ref, tsl_ref, m_ref,
             square_ref, modes_ref, load_ref, sems):
        def moves(r, columns, k):
            return [
                pltpu.make_async_copy(source, target.at[r], sems.at[i, k])
                for i, (source, target) in enumerate((
                    (s_hbm.at[r, columns], square_ref), (modes_hbm.at[r], modes_ref), (load_hbm.at[r], load_ref)
                ))
            ]

        for k in range(order // b):
            for move in moves(pl.ds(k * b, b), pl.ds(k * b, b), k):
                move.start()
        index = jnp.concatenate(row_sides(me_ref, l_ref, r_ref), axis=1)
        mask = jnp.where(lax.broadcasted_iota(jnp.int32, (1, nm), 1) < count_ref[0], 1.0, 0.0)
        eye = lax.broadcasted_iota(jnp.int32, (b, b), 0) == lax.broadcasted_iota(jnp.int32, (b, b), 1)
        lane = lax.broadcasted_iota(jnp.int32, (b, 128), 1)

        def step(r, start, carry):
            shared, weights, modal = carry
            for move in moves(r, r, start // b):
                move.wait()
            row_id = lax.broadcasted_iota(jnp.int32, (b, two), 0) + start
            found = jnp.where(index == row_id, 1.0, 0.0)
            gt = found.astype(BF16)
            gt_ref[r] = gt
            live = jnp.where(lax.broadcasted_iota(jnp.int32, (b, 1), 0) + start < rows_ref[0], 1.0, 0.0)
            share = live / (1.0 + jnp.sum(found, axis=1, keepdims=True))
            diag = jnp.sum(jnp.where(eye, square_ref[r], 0.0), axis=1, keepdims=True)
            sd = share / diag
            weights = weights + jnp.sum(found * sd, axis=0, keepdims=True)
            vec_ref[r] = jnp.where(lane == 0, live, sd)
            phi = share * (modes_ref[r] * mask)
            ph_ref[r], pl_ref[r] = split2(phi)
            parts = split3(phi.T)
            pth_ref[:, r], ptl_ref[:, r] = parts[:2]
            shared = shared + mm(jnp.concatenate(parts, 1), jnp.concatenate([gt] * 3, 0))
            return shared, weights, modal + mm3(parts[:2], split2(load_ref[r]))

        shared, weights, modal = over_blocks(
            order, step, (jnp.zeros((nm, two), F32), jnp.zeros((1, two), F32), jnp.zeros((nm, k_load), F32))
        )
        m_ref[:nm] = modal
        m_ref[nm:] = jnp.zeros((SUMS, k_load), F32)
        tsh_ref[...], tsl_ref[...] = split2(shared)
        back = shared.T
        for i, ref in enumerate((x_ref, d_ref)):
            ref[:half] = back[i * half:(i + 1) * half]
            for t in range(pieces):
                at = i * half + t * nm
                ref[half + 8 * t:half + 8 * t + 8] = jnp.broadcast_to(weights[:, at:at + nm], (8, nm))

    half_type = dict(dtype=BF16)
    return call(
        body, [left, right],
        [shape(order, two, **half_type), shape(order, nm, **half_type), shape(order, nm, **half_type),
         shape(nm, order, **half_type), shape(nm, order, **half_type), shape(order, 128),
         shape(tall, nm), shape(tall, nm), shape(nm, two, **half_type), shape(nm, two, **half_type),
         shape(nm + SUMS, k_load)],
        6 * two * order * nm, [me, live_rows, live_modes], raw=[schur, modes, load], mb=14,
        scratch=[pltpu.VMEM((order, b), F32), pltpu.VMEM((order, nm), F32), pltpu.VMEM((order, k_load), F32),
                 pltpu.SemaphoreType.DMA((3, order // b))],
    )


def extend(onehot_t, vec, load, recv, phi_recv):
    order, two = onehot_t.shape
    half = two // 2
    k = load.shape[1]
    nm = phi_recv[0].shape[1]
    pieces = half // nm

    def body(gt_ref, vec_ref, f_ref, rx_ref, rd_ref, px_ref, pd_ref, r_ref, w_ref, nh_ref, nl_ref):
        field = [jnp.concatenate(p, 0) for p in zip(split2(rx_ref[...]), split2(rd_ref[...]))]
        weights = jnp.concatenate(
            [ref[half + 8 * t:half + 8 * t + 1] for ref in (px_ref, pd_ref) for t in range(pieces)], axis=1
        )
        modes = [jnp.concatenate(split2(ref[:half]), 0) for ref in (px_ref, pd_ref)]

        def step(r, _, carry):
            gt = gt_ref[r]
            w = vec_ref[r, 1:2] + jnp.sum(gt.astype(F32) * weights, axis=1, keepdims=True)
            w_ref[r] = jnp.broadcast_to(w, (w.shape[0], 128))
            r_ref[r] = vec_ref[r, 0:1] * f_ref[r] + pick(gt, field)
            for i in range(2):
                side = gt[:, i * half:(i + 1) * half]
                part = mm(jnp.concatenate([side, side], 1), modes[i])
                nh_ref[r, i * nm:(i + 1) * nm], nl_ref[r, i * nm:(i + 1) * nm] = split2(part)
            return carry

        over_blocks(order, step)

    return call(
        body, [onehot_t, vec, load, *recv, *phi_recv],
        [shape(order, k), shape(order, 128)] + [shape(order, 2 * nm, dtype=BF16)] * 2,
        2 * order * two * (3 * k + 2 * nm), mb=12,
    )


def schur_modes(schur, modes, after=()):
    order, n = modes[0].shape

    def body(s_ref, h_ref, l_ref, q_ref):
        rhs = (h_ref[...], l_ref[...])

        def block(r, _, carry):
            q_ref[r] = mm3(split2(s_ref[r]), rhs)
            return carry

        over_blocks(order, block, unroll=True)

    return call(body, [schur, *modes], [shape(order, n)], 6 * order * order * n, mb=10, after=after)[0]


def schur_apply(schur, x):
    order, k = x[0].shape

    def body(s_ref, xh_ref, xl_ref, y_ref):
        x = (xh_ref[...], xl_ref[...])

        def block(r, _, carry):
            y_ref[r] = mm3(split2(s_ref[r]), x)
            return carry

        over_blocks(order, block, unroll=True)

    return call(body, [schur, *x], [shape(order, k)], 6 * order * order * k, mb=10)[0]


def coarse(me, inverses, modal, after):
    nm, co = inverses[0].shape
    _, k = modal[0].shape
    n = len(modal)
    ordered = direct(2 * n)

    def body(me_ref, own_ref, x_ref, d_ref, z_ref, *rest):
        send_ref, keep_ref, d_out, z_out, xh, xl = rest[n:]
        pos = me_ref[0] // 2
        sums = jnp.zeros((SUMS, k), F32)
        for d in range(n):
            at = pl.ds(pl.multiple_of(((pos ^ d) if ordered else d) * nm, nm), nm)
            xh[at], xl[at] = split2(rest[d][:nm])
            sums = sums + rest[d][nm:]
        a = split2(jnp.concatenate([own_ref[...], x_ref[...], d_ref[...], z_ref[...]], 0))
        part = mm3(a, (xh[...], xl[...]))
        keep_ref[:3 * nm] = part[:3 * nm]
        keep_ref[3 * nm:] = sums
        send_ref[:nm] = part[nm:2 * nm]
        send_ref[nm:2 * nm] = part[:nm]
        send_ref[2 * nm:3 * nm] = part[3 * nm:]
        send_ref[3 * nm:] = sums
        d_out[...] = part[2 * nm:3 * nm]
        z_out[...] = part[3 * nm:]

    return call(
        body, [*inverses, *modal], [shape(3 * nm + SUMS, k)] * 2 + [shape(nm, k)] * 2,
        24 * nm * co * k, [me], scratch=[pltpu.VMEM((co, k), BF16)] * 2, mb=12, after=after,
    )


def whole_stack(me, last_sub, keep, recv, edges, out):
    nm = edges[0].shape[0]
    at_edge = jnp.logical_or(me == 0, me == last_sub)
    total = keep[:3 * nm] + recv[:3 * nm]
    out[:2 * nm] = total[:2 * nm]
    out[2 * nm:] = jnp.where(at_edge, edges[0][...] + edges[1][...], total[2 * nm:])


def first_direction(me, last_sub, keep, recv, edges, phi, phi_n, w, resid):
    order, nm = phi[0].shape
    k = resid.shape[1]

    def body(me_ref, keep_ref, recv_ref, e1_ref, e2_ref, h_ref, l_ref, nh_ref, nl_ref, w_ref, r_ref,
             st_ref, xh_ref, xl_ref):
        whole_stack(me_ref[0], last_sub, keep_ref, recv_ref, (e1_ref, e2_ref), st_ref)
        c = split2(st_ref[...])

        def step(r, _, carry):
            p = (jnp.concatenate([h_ref[r], nh_ref[r]], 1), jnp.concatenate([l_ref[r], nl_ref[r]], 1))
            xh_ref[r], xl_ref[r] = split2(mm3(p, c) + w_ref[r, 0:1] * r_ref[r])
            return carry

        over_blocks(order, step)

    return call(
        body, [keep, recv, *edges, *phi, *phi_n, w, resid],
        [shape(3 * nm, k)] + [shape(order, k, dtype=BF16)] * 2, 18 * order * nm * k, [me], mb=10,
    )


def first_image(y, vec, phi_t, resid):
    order, k = y.shape
    nm = phi_t[0].shape[0]

    def body(y_ref, vec_ref, th_ref, tl_ref, r_ref, p_ref, m_ref):
        def step(at, _, carry):
            num, den, modal = carry
            p = vec_ref[at, 0:1] * y_ref[at]
            p_ref[at] = p
            num = num + jnp.sum(r_ref[at] * p, axis=0, keepdims=True)
            den = den + jnp.sum(p * p, axis=0, keepdims=True)
            return num, den, modal + mm3((th_ref[:, at], tl_ref[:, at]), split2(p))

        zero = jnp.zeros((1, k), F32)
        num, den, modal = over_blocks(order, step, (zero, zero, jnp.zeros((nm, k), F32)))
        row = lax.broadcasted_iota(jnp.int32, (SUMS, k), 0)
        m_ref[:nm] = modal
        m_ref[nm:] = jnp.where(row == 0, num, jnp.where(row == 1, den, 0.0))

    return call(body, [y, vec, *phi_t, resid], [shape(order, k), shape(nm + SUMS, k)], 6 * nm * order * k, mb=8)


def shared_image(me, last_sub, left, right, order, q_shared, y_shared, keep, recv, edges):
    two = y_shared.shape[0]
    half = two // 2
    nm, k = edges[0].shape
    n = 3 * nm

    def body(me_ref, lv_ref, rv_ref, qo_ref, qn_ref, y_ref, keep_ref, recv_ref, e1_ref, e2_ref, x_ref, d_ref, st_ref):
        rows = row_sides(me_ref, lv_ref, rv_ref)
        whole_stack(me_ref[0], last_sub, keep_ref, recv_ref, (e1_ref, e2_ref), st_ref)
        c = split2(st_ref[...])
        for i, ref in enumerate((x_ref, d_ref)):
            at = slice(i * half, (i + 1) * half)
            found = y_ref[at] + mm3(split2(jnp.concatenate([qo_ref[at], qn_ref[at]], 1)), c)
            slot = lax.broadcasted_iota(jnp.int32, (half, k), 0)
            ref[...] = jnp.where(slot < used_count(rows[i], order), found, 0.0)

    return call(
        body, [left, right, *q_shared, y_shared, keep, recv, *edges],
        [shape(half, k)] * 2 + [shape(3 * nm, k)], 6 * two * n * k, [me], mb=10,
    )


def local_image(q, y, vec, phi_t, stack, chain, restrict):
    order = y.shape[0]
    n, k = stack.shape
    nm = phi_t[0].shape[0]

    def body(qo_ref, qn_ref, y_ref, vec_ref, th_ref, tl_ref, st_ref, *refs):
        ins, outs = refs[:len(chain)], list(refs[len(chain):])
        c = split2(st_ref[...])
        p_ref = outs.pop(0)
        r_ref = outs.pop(0)

        def step(at, _, carry):
            num, den, modal = carry
            p = vec_ref[at, 0:1] * (y_ref[at] + mm3(split2(jnp.concatenate([qo_ref[at], qn_ref[at]], 1)), c))
            scale = ins[1][0:1]
            p = ins[2][at] - scale * p
            r = ins[0][at] - scale * ins[3][at]
            r_ref[at] = r
            p_ref[at] = p
            num = num + jnp.sum(r * p, axis=0, keepdims=True)
            den = den + jnp.sum(p * p, axis=0, keepdims=True)
            if restrict:
                modal = modal + mm3((th_ref[:, at], tl_ref[:, at]), split2(p))
            return num, den, modal

        zero = jnp.zeros((1, k), F32)
        num, den, modal = over_blocks(order, step, (zero, zero, jnp.zeros((nm, k), F32)))
        row = lax.broadcasted_iota(jnp.int32, (SUMS, k), 0)
        m_ref = outs.pop(0)
        m_ref[:nm] = modal
        m_ref[nm:] = jnp.where(row == 0, num, jnp.where(row == 1, den, 0.0))

    outs = [shape(order, k)] * 2 + [shape(nm + SUMS, k)]
    return call(
        body, [*q, y, vec, *phi_t, stack, *chain], outs,
        6 * order * n * k + 6 * nm * order * k, mb=12,
    )


def finish(phi_ts, own, recv, sent=(), chain=(), after=()):
    nm, two = phi_ts[0].shape
    k = own.shape[1]
    plain = len(sent) == 0

    def body(h_ref, l_ref, m_ref, *refs):
        ins, outs = refs[:2 + len(sent) + len(chain)], refs[2 + len(sent) + len(chain):]
        got = jnp.concatenate([ins[0][...], ins[1][...]], 0)
        cross = jnp.zeros((1, k), F32)
        if not plain:
            put = jnp.concatenate([ins[2][...], ins[3][...]], 0)
            if chain:
                scale = ins[4][0:1]
                got = ins[5][...] - scale * got
                put = ins[6][...] - scale * put
            outs[1][...] = got
            outs[2][...] = put
            cross = jnp.sum(got * put, axis=0, keepdims=True)
        outs[0][:nm] = m_ref[:nm] + mm3((h_ref[...], l_ref[...]), split2(got))
        row = lax.broadcasted_iota(jnp.int32, (SUMS, k), 0)
        base = m_ref[nm:] if not plain else jnp.zeros((SUMS, k), F32)
        outs[0][nm:] = base + jnp.where(row == 1, cross, 0.0)

    outs = [shape(nm + SUMS, k)] + ([] if plain else [shape(two, k)] * 2)
    return call(body, [*phi_ts, own, *recv, *sent, *chain], outs, 6 * nm * two * k, mb=10, after=after)


def assemble(onehot_t, p, got, w=None):
    order, two = onehot_t.shape
    k = p.shape[1]

    def body(gt_ref, p_ref, g_ref, *refs):
        parts = jnp.concatenate(split2(g_ref[...]), 0)

        def step(r, _, carry):
            gt = gt_ref[r]
            new = p_ref[r] + mm(jnp.concatenate([gt, gt], 1), parts)
            if w is None:
                refs[0][r] = new
            else:
                w_ref, i_ref, xh_ref, xl_ref = refs
                i_ref[r] = new
                xh_ref[r], xl_ref[r] = split2(w_ref[r, 0:1] * new)
            return carry

        over_blocks(order, step)

    ins = [onehot_t, p, got] + ([] if w is None else [w])
    outs = [shape(order, k)] + ([] if w is None else [shape(order, k, dtype=BF16)] * 2)
    return call(body, ins, outs, 4 * order * two * k, mb=10)


def directions(phi, phi_n, w, scales, resids, stacks):
    order, _ = phi[0].shape
    n, k = stacks[0].shape

    def body(h_ref, l_ref, nh_ref, nl_ref, w_ref, a0_ref, a1_ref, r0_ref, r1_ref, r2_ref,
             c0_ref, e0_ref, e1_ref, sol_ref, dir_ref):
        s0, s1 = a0_ref[0:1], a1_ref[0:1]
        c0 = c0_ref[...]
        c1 = c0 - s0 * e0_ref[...]
        first = s0 * c0 + s1 * c1
        c = split2(jnp.concatenate([first, c1 - s1 * e1_ref[...]], 1))

        def step(r, _, carry):
            p = (jnp.concatenate([h_ref[r], nh_ref[r]], 1), jnp.concatenate([l_ref[r], nl_ref[r]], 1))
            both = mm3(p, c)
            wc = w_ref[r, 0:1]
            sol_ref[r] = both[:, :k] + wc * (s0 * r0_ref[r] + s1 * r1_ref[r])
            dir_ref[r] = both[:, k:] + wc * r2_ref[r]
            return carry

        over_blocks(order, step)

    return call(
        body, [*phi, *phi_n, w, *scales, *resids, *stacks], [shape(order, k)] * 2,
        12 * order * n * k, mb=12,
    )


def swap_x(value):
    n = lax.axis_size("sub")
    return lax.ppermute(value, "sub", [(i, i ^ 1) for i in range(n)])


def swap_d(value):
    n = lax.axis_size(BOTH)
    pairs = [(i, i + 1) for i in range(1, n - 1, 2)]
    return lax.ppermute(value, BOTH, pairs + [(b, a) for a, b in pairs])


def coarse_rows(me, inverse, after):
    n = lax.axis_size("sub")
    same, other = halves(me, inverse, after)
    ring = [((i + 1) % n, (i + 2) % n) for i in range(0, n, 2)]
    at_d = lax.ppermute(other, "sub", ring + [(b, a) for a, b in ring])
    at_x = swap_x(other)
    at_z = lax.ppermute(same, "sub", [(i, (i - 2) % n if i % 2 == 0 else (i + 2) % n) for i in range(n)])
    return same, at_x, at_d, at_z


def direct(n):
    return n & (n - 1) == 0 and n <= 8


def parity_blocks(modal):
    n = lax.axis_size("sub")
    if not direct(n):
        groups = [list(range(p, n, 2)) for p in range(2)]
        every = lax.all_gather(modal, "sub", axis=0, axis_index_groups=groups)
        return [every[d] for d in range(n // 2)]
    return [modal] + [
        lax.ppermute(modal, "sub", [(i, i ^ (2 * d)) for i in range(n)]) for d in range(1, n // 2)
    ]


def over_axis(value, axis):
    n = lax.axis_size(axis)
    if n & (n - 1):
        return lax.psum(value, axis)
    step = 1
    while step < n:
        value = value + lax.ppermute(value, axis, [(i, i ^ step) for i in range(n)])
        step *= 2
    return value


def edge_blocks(block, partner):
    n, m = lax.axis_size("sub"), lax.axis_size("cluster")
    out = []
    for value, shift in ((block, 0), (partner, 1)):
        up = [(n * c + shift, n * (c + 1)) for c in range(m - 1)]
        down = [(n * (c + 1) + n - 1 - shift, n * c + n - 1) for c in range(m - 1)]
        out.append(lax.ppermute(value, BOTH, up + down))
    return out


def scale_of(sums):
    value = sums[0:1] / (sums[1:2] + 1e-06)
    return jnp.broadcast_to(value, (8, value.shape[1]))


def program(load, schur, modes, coarse_inverse, interface_rows, mode_count, left_rows, right_rows):
    nm = modes.shape[1]
    n_sub = lax.axis_size("sub")
    me = lax.axis_index("sub").astype(jnp.int32).reshape(1)

    to_x, to_d = gather_load(me, left_rows, right_rows, load)
    recv = swap_x(to_x), swap_d(to_d)
    onehot_t, p_hi, p_lo, pt_hi, pt_lo, vec, phi_x, phi_d, ts_hi, ts_lo, own = prepare(
        me, interface_rows, mode_count, left_rows, right_rows, schur, modes, load
    )
    phi, phi_t, phi_ts = (p_hi, p_lo), (pt_hi, pt_lo), (ts_hi, ts_lo)
    inverses = coarse_rows(me, coarse_inverse, (own,))
    phi_recv = swap_x(phi_x), swap_d(phi_d)
    (modal,) = finish(phi_ts, own, recv)
    blocks = parity_blocks(modal)
    q_own = schur_modes(schur, phi, (modal,))
    resid, w, n_hi, n_lo = extend(onehot_t, vec, load, recv, phi_recv)
    phi_n = (n_hi, n_lo)

    scales, resids, stacks = [], [resid], []
    for iteration in range(ITERS):
        first, last = iteration == 0, iteration == ITERS - 1
        send, keep, end_d, end_z = coarse(me, inverses, blocks, (q_own,) if first else (y,))
        got = swap_x(send)
        edges = edge_blocks(end_d, end_z)
        if first:
            stack, x_hi, x_lo = first_direction(me, n_sub - 1, keep, got, edges, phi, phi_n, w, resid)
            y = schur_apply(schur, (x_hi, x_lo))
            to_x, to_d = gather_shared(me, left_rows, right_rows, [y], True)
        else:
            (y_shared,) = gather_shared(me, left_rows, right_rows, [y])
            to_x, to_d, stack = shared_image(
                me, n_sub - 1, left_rows, right_rows, schur.shape[0], q_shared, y_shared, keep, got, edges
            )
        stacks.append(stack)
        recv = swap_x(to_x), swap_d(to_d)
        if first:
            p, own = first_image(y, vec, phi_t, resid)
            q = (q_own, schur_modes(schur, phi_n))
            q_shared = gather_shared(me, left_rows, right_rows, list(q))
            modal, far, near = finish(phi_ts, own, recv, (to_x, to_d), (), tuple(q_shared))
        else:
            scale = scale_of(over_axis(keep[3 * nm:] + got[3 * nm:], "cluster"))
            scales.append(scale)
            p, resid, own = local_image(q, y, vec, phi_t, stack, (resid, scale, p, image), not last)
            resids.append(resid)
            early = ()
            if last:
                early = sol, final = directions(phi, phi_n, w, scales, resids, stacks)
            modal, far, near = finish(phi_ts, own, recv, (to_x, to_d), (scale, far, near), early)
        if not last:
            blocks = parity_blocks(modal)
            image, x_hi, x_lo = assemble(onehot_t, p, far, w)
            y = schur_apply(schur, (x_hi, x_lo))
    sums = over_axis(over_axis(modal[nm:], "cluster"), "sub")
    (image,) = assemble(onehot_t, p, far)
    scale = scale_of(sums)[0:1]
    return sol + scale * final, resid - scale * image


def solution(mesh):
    rows = P(BOTH, None)
    return jax.shard_map(
        program,
        mesh=mesh,
        in_specs=(rows, rows, rows, rows, P(BOTH), P(BOTH), rows, rows),
        out_specs=(rows, rows),
        check_vma=False,
    )
```

```python
import jax
import jax.numpy as jnp
from jax import lax
from jax.experimental import pallas as pl
from jax.experimental.pallas import tpu as pltpu
from jax.sharding import PartitionSpec as P


BOTH = ("cluster", "sub")
F32 = jnp.float32
BF16 = jnp.bfloat16
ITERS = 3
INTERPRET = False
SUMS = 8


def split2(x):
    hi = x.astype(BF16)
    return hi, (x - hi.astype(F32)).astype(BF16)


def split3(x):
    hi = x.astype(BF16)
    rest = x - hi.astype(F32)
    mid = rest.astype(BF16)
    return hi, mid, (rest - mid.astype(F32)).astype(BF16)


def mm(a, b):
    return jnp.dot(a, b, preferred_element_type=F32)


def mm3(a, b):
    return mm(jnp.concatenate([a[0], a[0]], 1), jnp.concatenate([b[0], b[1]], 0)) + mm(a[1], b[0])


def pick(onehot, parts):
    return mm(jnp.concatenate([onehot] * len(parts), 1), jnp.concatenate(parts, 0))


def shape(*dims, dtype=F32):
    return jax.ShapeDtypeStruct(dims, dtype)


def call(body, ins, outs, flops, scalars=(), scratch=(), mb=8, raw=(), after=()):
    moved = sum(a.size * a.dtype.itemsize for a in (*ins, *outs))
    lead = len(scalars) + len(raw) + len(ins)

    def run(*refs):
        body(*refs[:lead], *refs[lead + len(after):])

    anywhere = pl.BlockSpec(memory_space=pl.ANY)
    outside = pl.BlockSpec(memory_space=pltpu.HBM)
    on_chip = pl.BlockSpec(memory_space=pltpu.VMEM)
    return pl.pallas_call(
        run,
        in_specs=[pl.BlockSpec(memory_space=pltpu.SMEM)] * len(scalars) + [outside] * len(raw)
        + [on_chip] * len(ins) + [anywhere] * len(after),
        out_specs=[on_chip] * len(outs),
        out_shape=list(outs),
        scratch_shapes=list(scratch),
        cost_estimate=pl.CostEstimate(flops=int(flops), bytes_accessed=int(moved), transcendentals=0),
        compiler_params=pltpu.CompilerParams(vmem_limit_bytes=mb * 1024 * 1024),
        interpret=INTERPRET,
    )(*scalars, *[pltpu.with_memory_space_constraint(a, pltpu.HBM) for a in raw], *ins, *after)


def over_blocks(order, step, carry=0, unroll=False):
    b = block_of(order)
    if unroll:
        for k in range(0, order, b):
            carry = step(pl.ds(k, b), k, carry)
        return carry

    def one(k, carry):
        at = pl.multiple_of(k * b, b)
        return step(pl.ds(at, b), at, carry)

    return lax.fori_loop(0, order // b, one, carry)


def block_of(order):
    return 256 if order % 256 == 0 else order


def copy_rows(pairs, index_ref, base, half, order, masked):
    group = 8 if half % 8 == 0 else 1

    def step(j, _):
        for u in range(group):
            slot = j * group + u
            row = index_ref[0, slot]
            at = jnp.minimum(row, order - 1)
            for source, out in pairs:
                value = source[pl.ds(at, 1), :]
                out[pl.ds(base + slot, 1), :] = jnp.where(row < order, value, 0.0) if masked else value
        return 0

    lax.fori_loop(0, half // group, step, 0)


def by_parity(me, work):
    even = lax.rem(me, 2) == 0
    pl.when(even)(lambda: work(1, 0))
    pl.when(jnp.logical_not(even))(lambda: work(0, 1))


def row_sides(me_ref, left_ref, right_ref):
    even = lax.rem(me_ref[0], 2) == 0
    left, right = left_ref[...], right_ref[...]
    return jnp.where(even, right, left), jnp.where(even, left, right)


def used_count(row, order):
    return jnp.sum(jnp.where(row < order, 1, 0))


def gather_load(me, left, right, load):
    half = left.shape[1]
    order, k = load.shape

    def body(me_ref, l_hbm, r_hbm, load_hbm, x_ref, d_ref, l_ref, r_ref, load_ref, sems):
        moves = [
            pltpu.make_async_copy(source, target, sems.at[i])
            for i, (source, target) in enumerate(((l_hbm, l_ref), (r_hbm, r_ref), (load_hbm, load_ref)))
        ]
        for move in moves:
            move.start()
        for move in moves:
            move.wait()
        rows = (l_ref, r_ref)

        def work(first, second):
            copy_rows([(load_ref, x_ref)], rows[first], 0, half, order, True)
            copy_rows([(load_ref, d_ref)], rows[second], 0, half, order, True)

        by_parity(me_ref[0], work)

    return call(
        body, [], [shape(half, k)] * 2, 0, [me], raw=[left, right, load],
        scratch=[pltpu.SMEM((1, half), jnp.int32)] * 2 + [pltpu.VMEM((order, k), F32), pltpu.SemaphoreType.DMA((3,))],
    )


def gather_shared(me, left, right, fields):
    half = left.shape[1]
    order = fields[0].shape[0]
    n = len(fields)

    def body(me_ref, l_ref, r_ref, *refs):
        rows = (l_ref, r_ref)
        pairs = list(zip(refs[:n], refs[n:]))

        def work(first, second):
            copy_rows(pairs, rows[first], 0, half, order, False)
            copy_rows(pairs, rows[second], half, half, order, False)

        by_parity(me_ref[0], work)

    outs = [shape(2 * half, f.shape[1]) for f in fields]
    return call(body, fields, outs, 2e9, [me, left, right], mb=4)


def gather_side(me, left, right, field, side):
    half = left.shape[1]
    order, k = field.shape

    def body(me_ref, l_ref, r_ref, field_ref, out_ref):
        rows = (l_ref, r_ref)
        by_parity(
            me_ref[0], lambda *sides: copy_rows([(field_ref, out_ref)], rows[sides[side]], 0, half, order, True)
        )

    return call(body, [field], [shape(half, k)], 1e9, [me, left, right], mb=4)[0]


def halves(me, inverse, after):
    nm, co = inverse.shape

    def body(me_ref, c_ref, same_ref, other_ref):
        par = lax.rem(me_ref[0], 2)
        for j in range(co // nm // 2):
            to = slice(j * nm, (j + 1) * nm)
            same_ref[:, to] = c_ref[:, pl.ds(pl.multiple_of((2 * j + par) * nm, nm), nm)]
            other_ref[:, to] = c_ref[:, pl.ds(pl.multiple_of((2 * j + 1 - par) * nm, nm), nm)]

    return call(body, [inverse], [shape(nm, co // 2)] * 2, 0, [me], after=after)


def prepare(me, live_rows, live_modes, left, right, schur, modes, load):
    order, nm = modes.shape
    half = left.shape[1]
    two = 2 * half
    pieces = half // nm
    tall = half + 8 * pieces
    b = block_of(order)
    k_load = load.shape[1]

    def body(me_ref, rows_ref, count_ref, s_hbm, modes_hbm, load_hbm, l_ref, r_ref,
             gt_ref, ph_ref, pl_ref, pth_ref, ptl_ref, vec_ref, x_ref, d_ref, tsh_ref, tsl_ref, m_ref,
             square_ref, modes_ref, load_ref, sems):
        def moves(r, columns, k):
            return [
                pltpu.make_async_copy(source, target.at[r], sems.at[i, k])
                for i, (source, target) in enumerate((
                    (s_hbm.at[r, columns], square_ref), (modes_hbm.at[r], modes_ref), (load_hbm.at[r], load_ref)
                ))
            ]

        for k in range(order // b):
            for move in moves(pl.ds(k * b, b), pl.ds(k * b, b), k):
                move.start()
        index = jnp.concatenate(row_sides(me_ref, l_ref, r_ref), axis=1)
        mask = jnp.where(lax.broadcasted_iota(jnp.int32, (1, nm), 1) < count_ref[0], 1.0, 0.0)
        eye = lax.broadcasted_iota(jnp.int32, (b, b), 0) == lax.broadcasted_iota(jnp.int32, (b, b), 1)
        lane = lax.broadcasted_iota(jnp.int32, (b, 128), 1)

        def step(r, start, carry):
            shared, weights, modal = carry
            for move in moves(r, r, start // b):
                move.wait()
            row_id = lax.broadcasted_iota(jnp.int32, (b, two), 0) + start
            found = jnp.where(index == row_id, 1.0, 0.0)
            gt = found.astype(BF16)
            gt_ref[r] = gt
            live = jnp.where(lax.broadcasted_iota(jnp.int32, (b, 1), 0) + start < rows_ref[0], 1.0, 0.0)
            share = live / (1.0 + jnp.sum(found, axis=1, keepdims=True))
            diag = jnp.sum(jnp.where(eye, square_ref[r], 0.0), axis=1, keepdims=True)
            sd = share / diag
            weights = weights + jnp.sum(found * sd, axis=0, keepdims=True)
            vec_ref[r] = jnp.where(lane == 0, live, sd)
            phi = share * (modes_ref[r] * mask)
            ph_ref[r], pl_ref[r] = split2(phi)
            parts = split3(phi.T)
            pth_ref[:, r], ptl_ref[:, r] = parts[:2]
            shared = shared + mm(jnp.concatenate(parts, 1), jnp.concatenate([gt] * 3, 0))
            return shared, weights, modal + mm3(parts[:2], split2(load_ref[r]))

        shared, weights, modal = over_blocks(
            order, step, (jnp.zeros((nm, two), F32), jnp.zeros((1, two), F32), jnp.zeros((nm, k_load), F32))
        )
        m_ref[:nm] = modal
        m_ref[nm:] = jnp.zeros((SUMS, k_load), F32)
        tsh_ref[...], tsl_ref[...] = split2(shared)
        back = shared.T
        for i, ref in enumerate((x_ref, d_ref)):
            ref[:half] = back[i * half:(i + 1) * half]
            for t in range(pieces):
                at = i * half + t * nm
                ref[half + 8 * t:half + 8 * t + 8] = jnp.broadcast_to(weights[:, at:at + nm], (8, nm))

    half_type = dict(dtype=BF16)
    return call(
        body, [left, right],
        [shape(order, two, **half_type), shape(order, nm, **half_type), shape(order, nm, **half_type),
         shape(nm, order, **half_type), shape(nm, order, **half_type), shape(order, 128),
         shape(tall, nm), shape(tall, nm), shape(nm, two, **half_type), shape(nm, two, **half_type),
         shape(nm + SUMS, k_load)],
        6 * two * order * nm, [me, live_rows, live_modes], raw=[schur, modes, load], mb=14,
        scratch=[pltpu.VMEM((order, b), F32), pltpu.VMEM((order, nm), F32), pltpu.VMEM((order, k_load), F32),
                 pltpu.SemaphoreType.DMA((3, order // b))],
    )


def extend(onehot_t, vec, load, recv, phi_recv):
    order, two = onehot_t.shape
    half = two // 2
    k = load.shape[1]
    nm = phi_recv[0].shape[1]
    pieces = half // nm

    def body(gt_ref, vec_ref, f_ref, rx_ref, rd_ref, px_ref, pd_ref, r_ref, w_ref, nh_ref, nl_ref):
        field = [jnp.concatenate(p, 0) for p in zip(split2(rx_ref[...]), split2(rd_ref[...]))]
        weights = jnp.concatenate(
            [ref[half + 8 * t:half + 8 * t + 1] for ref in (px_ref, pd_ref) for t in range(pieces)], axis=1
        )
        modes = [jnp.concatenate(split2(ref[:half]), 0) for ref in (px_ref, pd_ref)]

        def step(r, _, carry):
            gt = gt_ref[r]
            w = vec_ref[r, 1:2] + jnp.sum(gt.astype(F32) * weights, axis=1, keepdims=True)
            w_ref[r] = jnp.broadcast_to(w, (w.shape[0], 128))
            r_ref[r] = vec_ref[r, 0:1] * f_ref[r] + pick(gt, field)
            for i in range(2):
                side = gt[:, i * half:(i + 1) * half]
                part = mm(jnp.concatenate([side, side], 1), modes[i])
                nh_ref[r, i * nm:(i + 1) * nm], nl_ref[r, i * nm:(i + 1) * nm] = split2(part)
            return carry

        over_blocks(order, step)

    return call(
        body, [onehot_t, vec, load, *recv, *phi_recv],
        [shape(order, k), shape(order, 128)] + [shape(order, 2 * nm, dtype=BF16)] * 2,
        2 * order * two * (3 * k + 2 * nm), mb=12,
    )


def schur_modes(schur, modes, after=()):
    order, n = modes[0].shape

    def body(s_ref, h_ref, l_ref, q_ref):
        rhs = (h_ref[...], l_ref[...])

        def block(r, _, carry):
            q_ref[r] = mm3(split2(s_ref[r]), rhs)
            return carry

        over_blocks(order, block, unroll=True)

    return call(body, [schur, *modes], [shape(order, n)], 6 * order * order * n, mb=10, after=after)[0]


def schur_apply(schur, x):
    order, k = x[0].shape

    def body(s_ref, xh_ref, xl_ref, y_ref):
        x = (xh_ref[...], xl_ref[...])

        def block(r, _, carry):
            y_ref[r] = mm3(split2(s_ref[r]), x)
            return carry

        over_blocks(order, block, unroll=True)

    return call(body, [schur, *x], [shape(order, k)], 6 * order * order * k, mb=10)[0]


def coarse(me, inverses, modal, after):
    nm, co = inverses[0].shape
    _, k = modal[0].shape
    n = len(modal)
    ordered = direct(2 * n)

    def body(me_ref, own_ref, x_ref, d_ref, z_ref, *rest):
        send_ref, keep_ref, d_out, z_out, xh, xl = rest[n:]
        pos = me_ref[0] // 2
        sums = jnp.zeros((SUMS, k), F32)
        for d in range(n):
            at = pl.ds(pl.multiple_of(((pos ^ d) if ordered else d) * nm, nm), nm)
            xh[at], xl[at] = split2(rest[d][:nm])
            sums = sums + rest[d][nm:]
        a = split2(jnp.concatenate([own_ref[...], x_ref[...], d_ref[...], z_ref[...]], 0))
        part = mm3(a, (xh[...], xl[...]))
        keep_ref[:3 * nm] = part[:3 * nm]
        keep_ref[3 * nm:] = sums
        send_ref[:nm] = part[nm:2 * nm]
        send_ref[nm:2 * nm] = part[:nm]
        send_ref[2 * nm:3 * nm] = part[3 * nm:]
        send_ref[3 * nm:] = sums
        d_out[...] = part[2 * nm:3 * nm]
        z_out[...] = part[3 * nm:]

    return call(
        body, [*inverses, *modal], [shape(3 * nm + SUMS, k)] * 2 + [shape(nm, k)] * 2,
        24 * nm * co * k, [me], scratch=[pltpu.VMEM((co, k), BF16)] * 2, mb=12, after=after,
    )


def whole_stack(me, last_sub, keep, recv, edges, out):
    nm = edges[0].shape[0]
    at_edge = jnp.logical_or(me == 0, me == last_sub)
    total = keep[:3 * nm] + recv[:3 * nm]
    out[:2 * nm] = total[:2 * nm]
    out[2 * nm:] = jnp.where(at_edge, edges[0][...] + edges[1][...], total[2 * nm:])


def first_direction(me, last_sub, keep, recv, edges, phi, phi_n, w, resid):
    order, nm = phi[0].shape
    k = resid.shape[1]

    def body(me_ref, keep_ref, recv_ref, e1_ref, e2_ref, h_ref, l_ref, nh_ref, nl_ref, w_ref, r_ref,
             st_ref, xh_ref, xl_ref):
        whole_stack(me_ref[0], last_sub, keep_ref, recv_ref, (e1_ref, e2_ref), st_ref)
        c = split2(st_ref[...])

        def step(r, _, carry):
            p = (jnp.concatenate([h_ref[r], nh_ref[r]], 1), jnp.concatenate([l_ref[r], nl_ref[r]], 1))
            xh_ref[r], xl_ref[r] = split2(mm3(p, c) + w_ref[r, 0:1] * r_ref[r])
            return carry

        over_blocks(order, step)

    return call(
        body, [keep, recv, *edges, *phi, *phi_n, w, resid],
        [shape(3 * nm, k)] + [shape(order, k, dtype=BF16)] * 2, 18 * order * nm * k, [me], mb=10,
    )


def first_image(y, vec, phi_t, resid):
    order, k = y.shape
    nm = phi_t[0].shape[0]

    def body(y_ref, vec_ref, th_ref, tl_ref, r_ref, p_ref, m_ref):
        def step(at, _, carry):
            num, den, modal = carry
            p = vec_ref[at, 0:1] * y_ref[at]
            p_ref[at] = p
            num = num + jnp.sum(r_ref[at] * p, axis=0, keepdims=True)
            den = den + jnp.sum(p * p, axis=0, keepdims=True)
            return num, den, modal + mm3((th_ref[:, at], tl_ref[:, at]), split2(p))

        zero = jnp.zeros((1, k), F32)
        num, den, modal = over_blocks(order, step, (zero, zero, jnp.zeros((nm, k), F32)))
        row = lax.broadcasted_iota(jnp.int32, (SUMS, k), 0)
        m_ref[:nm] = modal
        m_ref[nm:] = jnp.where(row == 0, num, jnp.where(row == 1, den, 0.0))

    return call(body, [y, vec, *phi_t, resid], [shape(order, k), shape(nm + SUMS, k)], 6 * nm * order * k, mb=8)


def shared_image(me, last_sub, left, right, order, q_shared, y_shared, keep, recv, edges):
    two = y_shared.shape[0]
    half = two // 2
    nm, k = edges[0].shape
    n = 3 * nm

    def body(me_ref, lv_ref, rv_ref, qo_ref, qn_ref, y_ref, keep_ref, recv_ref, e1_ref, e2_ref, x_ref, d_ref, st_ref):
        rows = row_sides(me_ref, lv_ref, rv_ref)
        whole_stack(me_ref[0], last_sub, keep_ref, recv_ref, (e1_ref, e2_ref), st_ref)
        c = split2(st_ref[...])
        for i, ref in enumerate((x_ref, d_ref)):
            at = slice(i * half, (i + 1) * half)
            found = y_ref[at] + mm3(split2(jnp.concatenate([qo_ref[at], qn_ref[at]], 1)), c)
            slot = lax.broadcasted_iota(jnp.int32, (half, k), 0)
            ref[...] = jnp.where(slot < used_count(rows[i], order), found, 0.0)

    return call(
        body, [left, right, *q_shared, y_shared, keep, recv, *edges],
        [shape(half, k)] * 2 + [shape(3 * nm, k)], 6 * two * n * k, [me], mb=10,
    )


def local_image(q, y, vec, phi_t, stack, chain, restrict):
    order = y.shape[0]
    n, k = stack.shape
    nm = phi_t[0].shape[0]

    def body(qo_ref, qn_ref, y_ref, vec_ref, th_ref, tl_ref, st_ref, *refs):
        ins, outs = refs[:len(chain)], list(refs[len(chain):])
        c = split2(st_ref[...])
        p_ref = outs.pop(0)
        r_ref = outs.pop(0)

        def step(at, _, carry):
            num, den, modal = carry
            p = vec_ref[at, 0:1] * (y_ref[at] + mm3(split2(jnp.concatenate([qo_ref[at], qn_ref[at]], 1)), c))
            scale = ins[1][0:1]
            p = ins[2][at] - scale * p
            r = ins[0][at] - scale * ins[3][at]
            r_ref[at] = r
            p_ref[at] = p
            num = num + jnp.sum(r * p, axis=0, keepdims=True)
            den = den + jnp.sum(p * p, axis=0, keepdims=True)
            if restrict:
                modal = modal + mm3((th_ref[:, at], tl_ref[:, at]), split2(p))
            return num, den, modal

        zero = jnp.zeros((1, k), F32)
        num, den, modal = over_blocks(order, step, (zero, zero, jnp.zeros((nm, k), F32)))
        row = lax.broadcasted_iota(jnp.int32, (SUMS, k), 0)
        m_ref = outs.pop(0)
        m_ref[:nm] = modal
        m_ref[nm:] = jnp.where(row == 0, num, jnp.where(row == 1, den, 0.0))

    outs = [shape(order, k)] * 2 + [shape(nm + SUMS, k)]
    return call(
        body, [*q, y, vec, *phi_t, stack, *chain], outs,
        6 * order * n * k + 6 * nm * order * k, mb=12,
    )


def finish(phi_ts, own, recv, sent=(), chain=(), after=()):
    nm, two = phi_ts[0].shape
    k = own.shape[1]
    plain = len(sent) == 0

    def body(h_ref, l_ref, m_ref, *refs):
        ins, outs = refs[:2 + len(sent) + len(chain)], refs[2 + len(sent) + len(chain):]
        got = jnp.concatenate([ins[0][...], ins[1][...]], 0)
        cross = jnp.zeros((1, k), F32)
        if not plain:
            put = jnp.concatenate([ins[2][...], ins[3][...]], 0)
            if chain:
                scale = ins[4][0:1]
                got = ins[5][...] - scale * got
                put = ins[6][...] - scale * put
            outs[1][...] = got
            outs[2][...] = put
            cross = jnp.sum(got * put, axis=0, keepdims=True)
        outs[0][:nm] = m_ref[:nm] + mm3((h_ref[...], l_ref[...]), split2(got))
        row = lax.broadcasted_iota(jnp.int32, (SUMS, k), 0)
        base = m_ref[nm:] if not plain else jnp.zeros((SUMS, k), F32)
        outs[0][nm:] = base + jnp.where(row == 1, cross, 0.0)

    outs = [shape(nm + SUMS, k)] + ([] if plain else [shape(two, k)] * 2)
    return call(body, [*phi_ts, own, *recv, *sent, *chain], outs, 6 * nm * two * k, mb=10, after=after)


def assemble(onehot_t, p, got, w=None):
    order, two = onehot_t.shape
    k = p.shape[1]

    def body(gt_ref, p_ref, g_ref, *refs):
        parts = jnp.concatenate(split2(g_ref[...]), 0)

        def step(r, _, carry):
            gt = gt_ref[r]
            new = p_ref[r] + mm(jnp.concatenate([gt, gt], 1), parts)
            if w is None:
                refs[0][r] = new
            else:
                w_ref, i_ref, xh_ref, xl_ref = refs
                i_ref[r] = new
                xh_ref[r], xl_ref[r] = split2(w_ref[r, 0:1] * new)
            return carry

        over_blocks(order, step)

    ins = [onehot_t, p, got] + ([] if w is None else [w])
    outs = [shape(order, k)] + ([] if w is None else [shape(order, k, dtype=BF16)] * 2)
    return call(body, ins, outs, 4 * order * two * k, mb=10)


def directions(phi, phi_n, w, scales, resids, stacks):
    order, _ = phi[0].shape
    n, k = stacks[0].shape

    def body(h_ref, l_ref, nh_ref, nl_ref, w_ref, a0_ref, a1_ref, r0_ref, r1_ref, r2_ref,
             c0_ref, e0_ref, e1_ref, sol_ref, dir_ref):
        s0, s1 = a0_ref[0:1], a1_ref[0:1]
        c0 = c0_ref[...]
        c1 = c0 - s0 * e0_ref[...]
        first = s0 * c0 + s1 * c1
        c = split2(jnp.concatenate([first, c1 - s1 * e1_ref[...]], 1))

        def step(r, _, carry):
            p = (jnp.concatenate([h_ref[r], nh_ref[r]], 1), jnp.concatenate([l_ref[r], nl_ref[r]], 1))
            both = mm3(p, c)
            wc = w_ref[r, 0:1]
            sol_ref[r] = both[:, :k] + wc * (s0 * r0_ref[r] + s1 * r1_ref[r])
            dir_ref[r] = both[:, k:] + wc * r2_ref[r]
            return carry

        over_blocks(order, step)

    return call(
        body, [*phi, *phi_n, w, *scales, *resids, *stacks], [shape(order, k)] * 2,
        12 * order * n * k, mb=12,
    )


def swap_x(value):
    n = lax.axis_size("sub")
    return lax.ppermute(value, "sub", [(i, i ^ 1) for i in range(n)])


def swap_d(value):
    n = lax.axis_size(BOTH)
    pairs = [(i, i + 1) for i in range(1, n - 1, 2)]
    return lax.ppermute(value, BOTH, pairs + [(b, a) for a, b in pairs])


def coarse_rows(me, inverse, after):
    n = lax.axis_size("sub")
    same, other = halves(me, inverse, after)
    at_z = lax.ppermute(same, "sub", [(i, (i - 2) % n if i % 2 == 0 else (i + 2) % n) for i in range(n)])
    return same, at_z, other


def coarse_partners(other):
    n = lax.axis_size("sub")
    ring = [((i + 1) % n, (i + 2) % n) for i in range(0, n, 2)]
    return swap_x(other), lax.ppermute(other, "sub", ring + [(b, a) for a, b in ring])


def direct(n):
    return n & (n - 1) == 0 and n <= 8


def parity_blocks(modal):
    n = lax.axis_size("sub")
    if not direct(n):
        groups = [list(range(p, n, 2)) for p in range(2)]
        every = lax.all_gather(modal, "sub", axis=0, axis_index_groups=groups)
        return [every[d] for d in range(n // 2)]
    return [modal] + [
        lax.ppermute(modal, "sub", [(i, i ^ (2 * d)) for i in range(n)]) for d in range(1, n // 2)
    ]


def over_axis(value, axis):
    n = lax.axis_size(axis)
    if n & (n - 1):
        return lax.psum(value, axis)
    step = 1
    while step < n:
        value = value + lax.ppermute(value, axis, [(i, i ^ step) for i in range(n)])
        step *= 2
    return value


def over_mesh(value):
    m, n = lax.axis_size("cluster"), lax.axis_size("sub")
    if m < 4 or n < 2 or m & (m - 1) or n & (n - 1):
        return over_axis(over_axis(value, "cluster"), "sub")
    value = value + lax.ppermute(value, "cluster", [(i, i ^ 1) for i in range(m)])
    here = [(c, s) for c in range(m) for s in range(n)]
    round_of = [(2, 0), (0, 1), (2, 1)]
    got = [
        lax.ppermute(value, BOTH, [(c * n + s, (c ^ up) * n + (s ^ along)) for c, s in here])
        for up, along in round_of
    ]
    value = (value + got[0]) + (got[1] + got[2])
    for step in [4 << i for i in range(8) if 4 << i < m]:
        value = value + lax.ppermute(value, "cluster", [(i, i ^ step) for i in range(m)])
    for step in [2 << i for i in range(8) if 2 << i < n]:
        value = value + lax.ppermute(value, "sub", [(i, i ^ step) for i in range(n)])
    return value


def edge_blocks(block, partner):
    n, m = lax.axis_size("sub"), lax.axis_size("cluster")
    out = []
    for value, shift in ((block, 0), (partner, 1)):
        up = [(n * c + shift, n * (c + 1)) for c in range(m - 1)]
        down = [(n * (c + 1) + n - 1 - shift, n * c + n - 1) for c in range(m - 1)]
        out.append(lax.ppermute(value, BOTH, up + down))
    return out


def scale_of(sums):
    value = sums[0:1] / (sums[1:2] + 1e-06)
    return jnp.broadcast_to(value, (8, value.shape[1]))


def program(load, schur, modes, coarse_inverse, interface_rows, mode_count, left_rows, right_rows):
    nm = modes.shape[1]
    n_sub = lax.axis_size("sub")
    me = lax.axis_index("sub").astype(jnp.int32).reshape(1)

    to_x, to_d = gather_load(me, left_rows, right_rows, load)
    recv = swap_x(to_x), swap_d(to_d)
    onehot_t, p_hi, p_lo, pt_hi, pt_lo, vec, phi_x, phi_d, ts_hi, ts_lo, own = prepare(
        me, interface_rows, mode_count, left_rows, right_rows, schur, modes, load
    )
    phi, phi_t, phi_ts = (p_hi, p_lo), (pt_hi, pt_lo), (ts_hi, ts_lo)
    rows_own, rows_z, other = coarse_rows(me, coarse_inverse, (own,))
    q_own = schur_modes(schur, phi)
    (modal,) = finish(phi_ts, own, recv, after=(q_own,))
    blocks = parity_blocks(modal)
    other, _ = lax.optimization_barrier((other, modal))
    inverses = (rows_own, *coarse_partners(other), rows_z)
    phi_recv = swap_x(phi_x), swap_d(phi_d)
    resid, w, n_hi, n_lo = extend(onehot_t, vec, load, recv, phi_recv)
    phi_n = (n_hi, n_lo)

    scales, resids, stacks = [], [resid], []
    for iteration in range(ITERS):
        first, last = iteration == 0, iteration == ITERS - 1
        send, keep, end_d, end_z = coarse(me, inverses, blocks, () if first else (y,))
        got = swap_x(send)
        edges = edge_blocks(end_d, end_z)
        if first:
            stack, x_hi, x_lo = first_direction(me, n_sub - 1, keep, got, edges, phi, phi_n, w, resid)
            y = schur_apply(schur, (x_hi, x_lo))
            to_x = gather_side(me, left_rows, right_rows, y, 0)
            to_d = gather_side(me, left_rows, right_rows, y, 1)
        else:
            (y_shared,) = gather_shared(me, left_rows, right_rows, [y])
            to_x, to_d, stack = shared_image(
                me, n_sub - 1, left_rows, right_rows, schur.shape[0], q_shared, y_shared, keep, got, edges
            )
        stacks.append(stack)
        from_x = swap_x(to_x)
        recv = from_x, swap_d(to_d)
        if first:
            p, own = first_image(y, vec, phi_t, resid)
            q = (q_own, schur_modes(schur, phi_n))
            q_shared = gather_shared(me, left_rows, right_rows, list(q))
            modal, far, near = finish(phi_ts, own, recv, (to_x, to_d), (), tuple(q_shared))
        else:
            scale = scale_of(over_axis(keep[3 * nm:] + got[3 * nm:], "cluster"))
            scales.append(scale)
            p, resid, own = local_image(q, y, vec, phi_t, stack, (resid, scale, p, image), not last)
            resids.append(resid)
            early = ()
            if last:
                early = sol, final = directions(phi, phi_n, w, scales, resids, stacks)
            modal, far, near = finish(phi_ts, own, recv, (to_x, to_d), (scale, far, near), early)
        if not last:
            blocks = parity_blocks(modal)
            image, x_hi, x_lo = assemble(onehot_t, p, far, w)
            y = schur_apply(schur, (x_hi, x_lo))
    sums = over_mesh(modal[nm:])
    (image,) = assemble(onehot_t, p, far)
    scale = scale_of(sums)[0:1]
    return sol + scale * final, resid - scale * image


def solution(mesh):
    rows = P(BOTH, None)
    return jax.shard_map(
        program,
        mesh=mesh,
        in_specs=(rows, rows, rows, rows, P(BOTH), P(BOTH), rows, rows),
        out_specs=(rows, rows),
        check_vma=False,
    )
```

```python
import jax
import jax.numpy as jnp
from jax import lax
from jax.experimental import pallas as pl
from jax.experimental.pallas import tpu as pltpu
from jax.sharding import PartitionSpec as P


BOTH = ("cluster", "sub")
F32 = jnp.float32
BF16 = jnp.bfloat16
ITERS = 3
INTERPRET = False
SUMS = 8


def split2(x):
    hi = x.astype(BF16)
    return hi, (x - hi.astype(F32)).astype(BF16)


def split3(x):
    hi = x.astype(BF16)
    rest = x - hi.astype(F32)
    mid = rest.astype(BF16)
    return hi, mid, (rest - mid.astype(F32)).astype(BF16)


def mm(a, b):
    return jnp.dot(a, b, preferred_element_type=F32)


def mm3(a, b):
    return mm(jnp.concatenate([a[0], a[0]], 1), jnp.concatenate([b[0], b[1]], 0)) + mm(a[1], b[0])


def pick(onehot, parts):
    return mm(jnp.concatenate([onehot] * len(parts), 1), jnp.concatenate(parts, 0))


def shape(*dims, dtype=F32):
    return jax.ShapeDtypeStruct(dims, dtype)


def call(body, ins, outs, flops, scalars=(), scratch=(), mb=8, raw=(), after=()):
    moved = sum(a.size * a.dtype.itemsize for a in (*ins, *outs))
    lead = len(scalars) + len(raw) + len(ins)

    def run(*refs):
        body(*refs[:lead], *refs[lead + len(after):])

    anywhere = pl.BlockSpec(memory_space=pl.ANY)
    outside = pl.BlockSpec(memory_space=pltpu.HBM)
    on_chip = pl.BlockSpec(memory_space=pltpu.VMEM)
    return pl.pallas_call(
        run,
        in_specs=[pl.BlockSpec(memory_space=pltpu.SMEM)] * len(scalars) + [outside] * len(raw)
        + [on_chip] * len(ins) + [anywhere] * len(after),
        out_specs=[on_chip] * len(outs),
        out_shape=list(outs),
        scratch_shapes=list(scratch),
        cost_estimate=pl.CostEstimate(flops=int(flops), bytes_accessed=int(moved), transcendentals=0),
        compiler_params=pltpu.CompilerParams(vmem_limit_bytes=mb * 1024 * 1024),
        interpret=INTERPRET,
    )(*scalars, *[pltpu.with_memory_space_constraint(a, pltpu.HBM) for a in raw], *ins, *after)


def over_blocks(order, step, carry=0, unroll=False):
    b = block_of(order)
    if unroll:
        for k in range(0, order, b):
            carry = step(pl.ds(k, b), k, carry)
        return carry

    def one(k, carry):
        at = pl.multiple_of(k * b, b)
        return step(pl.ds(at, b), at, carry)

    return lax.fori_loop(0, order // b, one, carry)


def block_of(order):
    return 256 if order % 256 == 0 else order


def copy_rows(pairs, index_ref, base, half, order, masked):
    group = 8 if half % 8 == 0 else 1

    def step(j, _):
        rows = [index_ref[0, j * group + u] for u in range(group)]
        for source, out in pairs:
            values = [source[pl.ds(jnp.minimum(row, order - 1), 1), :] for row in rows]
            if masked:
                values = [jnp.where(row < order, value, 0.0) for row, value in zip(rows, values)]
            for u, value in enumerate(values):
                out[pl.ds(base + j * group + u, 1), :] = value
        return 0

    lax.fori_loop(0, half // group, step, 0)


def by_parity(me, work):
    even = lax.rem(me, 2) == 0
    pl.when(even)(lambda: work(1, 0))
    pl.when(jnp.logical_not(even))(lambda: work(0, 1))


def row_sides(me_ref, left_ref, right_ref):
    even = lax.rem(me_ref[0], 2) == 0
    left, right = left_ref[...], right_ref[...]
    return jnp.where(even, right, left), jnp.where(even, left, right)


def used_count(row, order):
    return jnp.sum(jnp.where(row < order, 1, 0))


def gather_load(me, left, right, load):
    half = left.shape[1]
    order, k = load.shape

    def body(me_ref, l_hbm, r_hbm, load_hbm, x_ref, d_ref, l_ref, r_ref, load_ref, sems):
        moves = [
            pltpu.make_async_copy(source, target, sems.at[i])
            for i, (source, target) in enumerate(((l_hbm, l_ref), (r_hbm, r_ref), (load_hbm, load_ref)))
        ]
        for move in moves:
            move.start()
        for move in moves:
            move.wait()
        rows = (l_ref, r_ref)

        def work(first, second):
            copy_rows([(load_ref, x_ref)], rows[first], 0, half, order, True)
            copy_rows([(load_ref, d_ref)], rows[second], 0, half, order, True)

        by_parity(me_ref[0], work)

    return call(
        body, [], [shape(half, k)] * 2, 0, [me], raw=[left, right, load],
        scratch=[pltpu.SMEM((1, half), jnp.int32)] * 2 + [pltpu.VMEM((order, k), F32), pltpu.SemaphoreType.DMA((3,))],
    )


def gather_shared(me, left, right, fields):
    half = left.shape[1]
    order = fields[0].shape[0]
    n = len(fields)

    def body(me_ref, l_ref, r_ref, *refs):
        rows = (l_ref, r_ref)
        pairs = list(zip(refs[:n], refs[n:]))

        def work(first, second):
            copy_rows(pairs, rows[first], 0, half, order, False)
            copy_rows(pairs, rows[second], half, half, order, False)

        by_parity(me_ref[0], work)

    outs = [shape(2 * half, f.shape[1]) for f in fields]
    return call(body, fields, outs, 2e9, [me, left, right], mb=4)


def gather_side(me, left, right, field, side):
    half = left.shape[1]
    order, k = field.shape

    def body(me_ref, l_ref, r_ref, field_ref, out_ref):
        rows = (l_ref, r_ref)
        by_parity(
            me_ref[0], lambda *sides: copy_rows([(field_ref, out_ref)], rows[sides[side]], 0, half, order, True)
        )

    return call(body, [field], [shape(half, k)], 1e9, [me, left, right], mb=4)[0]


def halves(me, inverse, after):
    nm, co = inverse.shape

    def body(me_ref, c_ref, same_ref, other_ref):
        par = lax.rem(me_ref[0], 2)
        for j in range(co // nm // 2):
            to = slice(j * nm, (j + 1) * nm)
            same_ref[:, to] = c_ref[:, pl.ds(pl.multiple_of((2 * j + par) * nm, nm), nm)]
            other_ref[:, to] = c_ref[:, pl.ds(pl.multiple_of((2 * j + 1 - par) * nm, nm), nm)]

    return call(body, [inverse], [shape(nm, co // 2)] * 2, 0, [me], after=after)


def prepare(me, live_rows, live_modes, left, right, schur, modes, load):
    order, nm = modes.shape
    half = left.shape[1]
    two = 2 * half
    pieces = half // nm
    tall = half + 8 * pieces
    b = block_of(order)
    k_load = load.shape[1]

    def body(me_ref, rows_ref, count_ref, s_hbm, modes_hbm, load_hbm, l_ref, r_ref,
             gt_ref, ph_ref, pl_ref, pth_ref, ptl_ref, vec_ref, x_ref, d_ref, tsh_ref, tsl_ref, m_ref,
             square_ref, modes_ref, load_ref, sems):
        def moves(r, columns, k):
            return [
                pltpu.make_async_copy(source, target.at[r], sems.at[i, k])
                for i, (source, target) in enumerate((
                    (s_hbm.at[r, columns], square_ref), (modes_hbm.at[r], modes_ref), (load_hbm.at[r], load_ref)
                ))
            ]

        for k in range(order // b):
            for move in moves(pl.ds(k * b, b), pl.ds(k * b, b), k):
                move.start()
        index = jnp.concatenate(row_sides(me_ref, l_ref, r_ref), axis=1)
        mask = jnp.where(lax.broadcasted_iota(jnp.int32, (1, nm), 1) < count_ref[0], 1.0, 0.0)
        eye = lax.broadcasted_iota(jnp.int32, (b, b), 0) == lax.broadcasted_iota(jnp.int32, (b, b), 1)
        lane = lax.broadcasted_iota(jnp.int32, (b, 128), 1)

        def step(r, start, carry):
            shared, weights, modal = carry
            for move in moves(r, r, start // b):
                move.wait()
            row_id = lax.broadcasted_iota(jnp.int32, (b, two), 0) + start
            found = jnp.where(index == row_id, 1.0, 0.0)
            gt = found.astype(BF16)
            gt_ref[r] = gt
            live = jnp.where(lax.broadcasted_iota(jnp.int32, (b, 1), 0) + start < rows_ref[0], 1.0, 0.0)
            share = live / (1.0 + jnp.sum(found, axis=1, keepdims=True))
            diag = jnp.sum(jnp.where(eye, square_ref[r], 0.0), axis=1, keepdims=True)
            sd = share / diag
            weights = weights + jnp.sum(found * sd, axis=0, keepdims=True)
            vec_ref[r] = jnp.where(lane == 0, live, sd)
            phi = share * (modes_ref[r] * mask)
            ph_ref[r], pl_ref[r] = split2(phi)
            parts = split3(phi.T)
            pth_ref[:, r], ptl_ref[:, r] = parts[:2]
            shared = shared + mm(jnp.concatenate(parts, 1), jnp.concatenate([gt] * 3, 0))
            return shared, weights, modal + mm3(parts[:2], split2(load_ref[r]))

        shared, weights, modal = over_blocks(
            order, step, (jnp.zeros((nm, two), F32), jnp.zeros((1, two), F32), jnp.zeros((nm, k_load), F32))
        )
        m_ref[:nm] = modal
        m_ref[nm:] = jnp.zeros((SUMS, k_load), F32)
        tsh_ref[...], tsl_ref[...] = split2(shared)
        back = shared.T
        for i, ref in enumerate((x_ref, d_ref)):
            ref[:half] = back[i * half:(i + 1) * half]
            for t in range(pieces):
                at = i * half + t * nm
                ref[half + 8 * t:half + 8 * t + 8] = jnp.broadcast_to(weights[:, at:at + nm], (8, nm))

    half_type = dict(dtype=BF16)
    return call(
        body, [left, right],
        [shape(order, two, **half_type), shape(order, nm, **half_type), shape(order, nm, **half_type),
         shape(nm, order, **half_type), shape(nm, order, **half_type), shape(order, 128),
         shape(tall, nm), shape(tall, nm), shape(nm, two, **half_type), shape(nm, two, **half_type),
         shape(nm + SUMS, k_load)],
        6 * two * order * nm, [me, live_rows, live_modes], raw=[schur, modes, load], mb=14,
        scratch=[pltpu.VMEM((order, b), F32), pltpu.VMEM((order, nm), F32), pltpu.VMEM((order, k_load), F32),
                 pltpu.SemaphoreType.DMA((3, order // b))],
    )


def extend(onehot_t, vec, load, recv, phi_recv):
    order, two = onehot_t.shape
    half = two // 2
    k = load.shape[1]
    nm = phi_recv[0].shape[1]
    pieces = half // nm

    def body(gt_ref, vec_ref, f_ref, rx_ref, rd_ref, px_ref, pd_ref, r_ref, w_ref, nh_ref, nl_ref):
        field = [jnp.concatenate(p, 0) for p in zip(split2(rx_ref[...]), split2(rd_ref[...]))]
        weights = jnp.concatenate(
            [ref[half + 8 * t:half + 8 * t + 1] for ref in (px_ref, pd_ref) for t in range(pieces)], axis=1
        )
        modes = [jnp.concatenate(split2(ref[:half]), 0) for ref in (px_ref, pd_ref)]

        def step(r, _, carry):
            gt = gt_ref[r]
            w = vec_ref[r, 1:2] + jnp.sum(gt.astype(F32) * weights, axis=1, keepdims=True)
            w_ref[r] = jnp.broadcast_to(w, (w.shape[0], 128))
            r_ref[r] = vec_ref[r, 0:1] * f_ref[r] + pick(gt, field)
            for i in range(2):
                side = gt[:, i * half:(i + 1) * half]
                part = mm(jnp.concatenate([side, side], 1), modes[i])
                nh_ref[r, i * nm:(i + 1) * nm], nl_ref[r, i * nm:(i + 1) * nm] = split2(part)
            return carry

        over_blocks(order, step)

    return call(
        body, [onehot_t, vec, load, *recv, *phi_recv],
        [shape(order, k), shape(order, 128)] + [shape(order, 2 * nm, dtype=BF16)] * 2,
        2 * order * two * (3 * k + 2 * nm), mb=12,
    )


def schur_modes(schur, modes, after=()):
    order, n = modes[0].shape

    def body(s_ref, h_ref, l_ref, q_ref):
        rhs = (h_ref[...], l_ref[...])

        def block(r, _, carry):
            q_ref[r] = mm3(split2(s_ref[r]), rhs)
            return carry

        over_blocks(order, block, unroll=True)

    return call(body, [schur, *modes], [shape(order, n)], 6 * order * order * n, mb=10, after=after)[0]


def schur_apply(schur, x):
    order, k = x[0].shape

    def body(s_ref, xh_ref, xl_ref, y_ref):
        x = (xh_ref[...], xl_ref[...])

        def block(r, _, carry):
            y_ref[r] = mm3(split2(s_ref[r]), x)
            return carry

        over_blocks(order, block, unroll=True)

    return call(body, [schur, *x], [shape(order, k)], 6 * order * order * k, mb=10)[0]


def coarse(me, inverses, modal, after):
    nm, co = inverses[0].shape
    _, k = modal[0].shape
    n = len(modal)
    ordered = direct(2 * n)

    def body(me_ref, own_ref, x_ref, d_ref, z_ref, *rest):
        send_ref, keep_ref, d_out, z_out, xh, xl = rest[n:]
        pos = me_ref[0] // 2
        sums = jnp.zeros((SUMS, k), F32)
        for d in range(n):
            at = pl.ds(pl.multiple_of(((pos ^ d) if ordered else d) * nm, nm), nm)
            xh[at], xl[at] = split2(rest[d][:nm])
            sums = sums + rest[d][nm:]
        a = split2(jnp.concatenate([own_ref[...], x_ref[...], d_ref[...], z_ref[...]], 0))
        part = mm3(a, (xh[...], xl[...]))
        keep_ref[:3 * nm] = part[:3 * nm]
        keep_ref[3 * nm:] = sums
        send_ref[:nm] = part[nm:2 * nm]
        send_ref[nm:2 * nm] = part[:nm]
        send_ref[2 * nm:3 * nm] = part[3 * nm:]
        send_ref[3 * nm:] = sums
        d_out[...] = part[2 * nm:3 * nm]
        z_out[...] = part[3 * nm:]

    return call(
        body, [*inverses, *modal], [shape(3 * nm + SUMS, k)] * 2 + [shape(nm, k)] * 2,
        24 * nm * co * k, [me], scratch=[pltpu.VMEM((co, k), BF16)] * 2, mb=12, after=after,
    )


def whole_stack(me, last_sub, keep, recv, edges, out):
    nm = edges[0].shape[0]
    at_edge = jnp.logical_or(me == 0, me == last_sub)
    total = keep[:3 * nm] + recv[:3 * nm]
    out[:2 * nm] = total[:2 * nm]
    out[2 * nm:] = jnp.where(at_edge, edges[0][...] + edges[1][...], total[2 * nm:])


def first_direction(me, last_sub, keep, recv, edges, phi, phi_n, w, resid):
    order, nm = phi[0].shape
    k = resid.shape[1]

    def body(me_ref, keep_ref, recv_ref, e1_ref, e2_ref, h_ref, l_ref, nh_ref, nl_ref, w_ref, r_ref,
             st_ref, xh_ref, xl_ref):
        whole_stack(me_ref[0], last_sub, keep_ref, recv_ref, (e1_ref, e2_ref), st_ref)
        c = split2(st_ref[...])

        def step(r, _, carry):
            p = (jnp.concatenate([h_ref[r], nh_ref[r]], 1), jnp.concatenate([l_ref[r], nl_ref[r]], 1))
            xh_ref[r], xl_ref[r] = split2(mm3(p, c) + w_ref[r, 0:1] * r_ref[r])
            return carry

        over_blocks(order, step)

    return call(
        body, [keep, recv, *edges, *phi, *phi_n, w, resid],
        [shape(3 * nm, k)] + [shape(order, k, dtype=BF16)] * 2, 18 * order * nm * k, [me], mb=10,
    )


def first_image(y, vec, phi_t, resid):
    order, k = y.shape
    nm = phi_t[0].shape[0]

    def body(y_ref, vec_ref, th_ref, tl_ref, r_ref, p_ref, m_ref):
        def step(at, _, carry):
            num, den, modal = carry
            p = vec_ref[at, 0:1] * y_ref[at]
            p_ref[at] = p
            num = num + jnp.sum(r_ref[at] * p, axis=0, keepdims=True)
            den = den + jnp.sum(p * p, axis=0, keepdims=True)
            return num, den, modal + mm3((th_ref[:, at], tl_ref[:, at]), split2(p))

        zero = jnp.zeros((1, k), F32)
        num, den, modal = over_blocks(order, step, (zero, zero, jnp.zeros((nm, k), F32)))
        row = lax.broadcasted_iota(jnp.int32, (SUMS, k), 0)
        m_ref[:nm] = modal
        m_ref[nm:] = jnp.where(row == 0, num, jnp.where(row == 1, den, 0.0))

    return call(body, [y, vec, *phi_t, resid], [shape(order, k), shape(nm + SUMS, k)], 6 * nm * order * k, mb=8)


def shared_image(me, last_sub, left, right, order, q_shared, y_shared, keep, recv, edges):
    two = y_shared.shape[0]
    half = two // 2
    nm, k = edges[0].shape
    n = 3 * nm

    def body(me_ref, lv_ref, rv_ref, qo_ref, qn_ref, y_ref, keep_ref, recv_ref, e1_ref, e2_ref, x_ref, d_ref, st_ref):
        rows = row_sides(me_ref, lv_ref, rv_ref)
        whole_stack(me_ref[0], last_sub, keep_ref, recv_ref, (e1_ref, e2_ref), st_ref)
        c = split2(st_ref[...])
        for i, ref in enumerate((x_ref, d_ref)):
            at = slice(i * half, (i + 1) * half)
            found = y_ref[at] + mm3(split2(jnp.concatenate([qo_ref[at], qn_ref[at]], 1)), c)
            slot = lax.broadcasted_iota(jnp.int32, (half, k), 0)
            ref[...] = jnp.where(slot < used_count(rows[i], order), found, 0.0)

    return call(
        body, [left, right, *q_shared, y_shared, keep, recv, *edges],
        [shape(half, k)] * 2 + [shape(3 * nm, k)], 6 * two * n * k, [me], mb=10,
    )


def local_image(q, y, vec, phi_t, stack, chain, restrict):
    order = y.shape[0]
    n, k = stack.shape
    nm = phi_t[0].shape[0]

    def body(qo_ref, qn_ref, y_ref, vec_ref, th_ref, tl_ref, st_ref, *refs):
        ins, outs = refs[:len(chain)], list(refs[len(chain):])
        c = split2(st_ref[...])
        p_ref = outs.pop(0)
        r_ref = outs.pop(0)

        def step(at, _, carry):
            num, den, modal = carry
            p = vec_ref[at, 0:1] * (y_ref[at] + mm3(split2(jnp.concatenate([qo_ref[at], qn_ref[at]], 1)), c))
            scale = ins[1][0:1]
            p = ins[2][at] - scale * p
            r = ins[0][at] - scale * ins[3][at]
            r_ref[at] = r
            p_ref[at] = p
            num = num + jnp.sum(r * p, axis=0, keepdims=True)
            den = den + jnp.sum(p * p, axis=0, keepdims=True)
            if restrict:
                modal = modal + mm3((th_ref[:, at], tl_ref[:, at]), split2(p))
            return num, den, modal

        zero = jnp.zeros((1, k), F32)
        num, den, modal = over_blocks(order, step, (zero, zero, jnp.zeros((nm, k), F32)))
        row = lax.broadcasted_iota(jnp.int32, (SUMS, k), 0)
        m_ref = outs.pop(0)
        m_ref[:nm] = modal
        m_ref[nm:] = jnp.where(row == 0, num, jnp.where(row == 1, den, 0.0))

    outs = [shape(order, k)] * 2 + [shape(nm + SUMS, k)]
    return call(
        body, [*q, y, vec, *phi_t, stack, *chain], outs,
        6 * order * n * k + 6 * nm * order * k, mb=12,
    )


def finish(phi_ts, own, recv, sent=(), chain=(), after=()):
    nm, two = phi_ts[0].shape
    k = own.shape[1]
    plain = len(sent) == 0

    def body(h_ref, l_ref, m_ref, *refs):
        ins, outs = refs[:2 + len(sent) + len(chain)], refs[2 + len(sent) + len(chain):]
        got = jnp.concatenate([ins[0][...], ins[1][...]], 0)
        cross = jnp.zeros((1, k), F32)
        if not plain:
            put = jnp.concatenate([ins[2][...], ins[3][...]], 0)
            if chain:
                scale = ins[4][0:1]
                got = ins[5][...] - scale * got
                put = ins[6][...] - scale * put
            outs[1][...] = got
            outs[2][...] = put
            cross = jnp.sum(got * put, axis=0, keepdims=True)
        outs[0][:nm] = m_ref[:nm] + mm3((h_ref[...], l_ref[...]), split2(got))
        row = lax.broadcasted_iota(jnp.int32, (SUMS, k), 0)
        base = m_ref[nm:] if not plain else jnp.zeros((SUMS, k), F32)
        outs[0][nm:] = base + jnp.where(row == 1, cross, 0.0)

    outs = [shape(nm + SUMS, k)] + ([] if plain else [shape(two, k)] * 2)
    return call(body, [*phi_ts, own, *recv, *sent, *chain], outs, 6 * nm * two * k, mb=10, after=after)


def assemble(onehot_t, p, got, w=None):
    order, two = onehot_t.shape
    k = p.shape[1]

    def body(gt_ref, p_ref, g_ref, *refs):
        parts = jnp.concatenate(split2(g_ref[...]), 0)

        def step(r, _, carry):
            gt = gt_ref[r]
            new = p_ref[r] + mm(jnp.concatenate([gt, gt], 1), parts)
            if w is None:
                refs[0][r] = new
            else:
                w_ref, i_ref, xh_ref, xl_ref = refs
                i_ref[r] = new
                xh_ref[r], xl_ref[r] = split2(w_ref[r, 0:1] * new)
            return carry

        over_blocks(order, step)

    ins = [onehot_t, p, got] + ([] if w is None else [w])
    outs = [shape(order, k)] + ([] if w is None else [shape(order, k, dtype=BF16)] * 2)
    return call(body, ins, outs, 4 * order * two * k, mb=10)


def directions(phi, phi_n, w, scales, resids, stacks):
    order, _ = phi[0].shape
    n, k = stacks[0].shape

    def body(h_ref, l_ref, nh_ref, nl_ref, w_ref, a0_ref, a1_ref, r0_ref, r1_ref, r2_ref,
             c0_ref, e0_ref, e1_ref, sol_ref, dir_ref):
        s0, s1 = a0_ref[0:1], a1_ref[0:1]
        c0 = c0_ref[...]
        c1 = c0 - s0 * e0_ref[...]
        first = s0 * c0 + s1 * c1
        c = split2(jnp.concatenate([first, c1 - s1 * e1_ref[...]], 1))

        def step(r, _, carry):
            p = (jnp.concatenate([h_ref[r], nh_ref[r]], 1), jnp.concatenate([l_ref[r], nl_ref[r]], 1))
            both = mm3(p, c)
            wc = w_ref[r, 0:1]
            sol_ref[r] = both[:, :k] + wc * (s0 * r0_ref[r] + s1 * r1_ref[r])
            dir_ref[r] = both[:, k:] + wc * r2_ref[r]
            return carry

        over_blocks(order, step)

    return call(
        body, [*phi, *phi_n, w, *scales, *resids, *stacks], [shape(order, k)] * 2,
        12 * order * n * k, mb=12,
    )


def swap_x(value):
    n = lax.axis_size("sub")
    return lax.ppermute(value, "sub", [(i, i ^ 1) for i in range(n)])


def swap_d(value):
    n = lax.axis_size(BOTH)
    pairs = [(i, i + 1) for i in range(1, n - 1, 2)]
    return lax.ppermute(value, BOTH, pairs + [(b, a) for a, b in pairs])


def coarse_rows(me, inverse, after):
    n = lax.axis_size("sub")
    same, other = halves(me, inverse, after)
    at_z = lax.ppermute(same, "sub", [(i, (i - 2) % n if i % 2 == 0 else (i + 2) % n) for i in range(n)])
    return same, at_z, other


def coarse_partners(other):
    n = lax.axis_size("sub")
    ring = [((i + 1) % n, (i + 2) % n) for i in range(0, n, 2)]
    return swap_x(other), lax.ppermute(other, "sub", ring + [(b, a) for a, b in ring])


def direct(n):
    return n & (n - 1) == 0 and n <= 8


def parity_blocks(modal):
    n = lax.axis_size("sub")
    if not direct(n):
        groups = [list(range(p, n, 2)) for p in range(2)]
        every = lax.all_gather(modal, "sub", axis=0, axis_index_groups=groups)
        return [every[d] for d in range(n // 2)]
    return [modal] + [
        lax.ppermute(modal, "sub", [(i, i ^ (2 * d)) for i in range(n)]) for d in range(1, n // 2)
    ]


def over_axis(value, axis):
    n = lax.axis_size(axis)
    if n & (n - 1):
        return lax.psum(value, axis)
    step = 1
    while step < n:
        value = value + lax.ppermute(value, axis, [(i, i ^ step) for i in range(n)])
        step *= 2
    return value


def over_mesh(value):
    m, n = lax.axis_size("cluster"), lax.axis_size("sub")
    if m < 4 or n < 2 or m & (m - 1) or n & (n - 1):
        return over_axis(over_axis(value, "cluster"), "sub")
    value = value + lax.ppermute(value, "cluster", [(i, i ^ 1) for i in range(m)])
    here = [(c, s) for c in range(m) for s in range(n)]
    round_of = [(2, 0), (0, 1), (2, 1)]
    got = [
        lax.ppermute(value, BOTH, [(c * n + s, (c ^ up) * n + (s ^ along)) for c, s in here])
        for up, along in round_of
    ]
    value = (value + got[0]) + (got[1] + got[2])
    for step in [4 << i for i in range(8) if 4 << i < m]:
        value = value + lax.ppermute(value, "cluster", [(i, i ^ step) for i in range(m)])
    for step in [2 << i for i in range(8) if 2 << i < n]:
        value = value + lax.ppermute(value, "sub", [(i, i ^ step) for i in range(n)])
    return value


def edge_blocks(block, partner):
    n, m = lax.axis_size("sub"), lax.axis_size("cluster")
    out = []
    for value, shift in ((block, 0), (partner, 1)):
        up = [(n * c + shift, n * (c + 1)) for c in range(m - 1)]
        down = [(n * (c + 1) + n - 1 - shift, n * c + n - 1) for c in range(m - 1)]
        out.append(lax.ppermute(value, BOTH, up + down))
    return out


def scale_of(sums):
    value = sums[0:1] / (sums[1:2] + 1e-06)
    return jnp.broadcast_to(value, (8, value.shape[1]))


def program(load, schur, modes, coarse_inverse, interface_rows, mode_count, left_rows, right_rows):
    nm = modes.shape[1]
    n_sub = lax.axis_size("sub")
    me = lax.axis_index("sub").astype(jnp.int32).reshape(1)

    to_x, to_d = gather_load(me, left_rows, right_rows, load)
    recv = swap_x(to_x), swap_d(to_d)
    onehot_t, p_hi, p_lo, pt_hi, pt_lo, vec, phi_x, phi_d, ts_hi, ts_lo, own = prepare(
        me, interface_rows, mode_count, left_rows, right_rows, schur, modes, load
    )
    phi, phi_t, phi_ts = (p_hi, p_lo), (pt_hi, pt_lo), (ts_hi, ts_lo)
    rows_own, rows_z, other = coarse_rows(me, coarse_inverse, (own,))
    q_own = schur_modes(schur, phi)
    (modal,) = finish(phi_ts, own, recv, after=(q_own,))
    blocks = parity_blocks(modal)
    other, _ = lax.optimization_barrier((other, modal))
    inverses = (rows_own, *coarse_partners(other), rows_z)
    phi_recv = swap_x(phi_x), swap_d(phi_d)
    resid, w, n_hi, n_lo = extend(onehot_t, vec, load, recv, phi_recv)
    phi_n = (n_hi, n_lo)

    scales, resids, stacks = [], [resid], []
    for iteration in range(ITERS):
        first, last = iteration == 0, iteration == ITERS - 1
        send, keep, end_d, end_z = coarse(me, inverses, blocks, () if first else (y,))
        got = swap_x(send)
        edges = edge_blocks(end_d, end_z)
        if first:
            stack, x_hi, x_lo = first_direction(me, n_sub - 1, keep, got, edges, phi, phi_n, w, resid)
            y = schur_apply(schur, (x_hi, x_lo))
            to_x = gather_side(me, left_rows, right_rows, y, 0)
            to_d = gather_side(me, left_rows, right_rows, y, 1)
        else:
            (y_shared,) = gather_shared(me, left_rows, right_rows, [y])
            to_x, to_d, stack = shared_image(
                me, n_sub - 1, left_rows, right_rows, schur.shape[0], q_shared, y_shared, keep, got, edges
            )
        stacks.append(stack)
        from_x = swap_x(to_x)
        recv = from_x, swap_d(to_d)
        if first:
            p, own = first_image(y, vec, phi_t, resid)
            q = (q_own, schur_modes(schur, phi_n))
            q_shared = gather_shared(me, left_rows, right_rows, list(q))
            modal, far, near = finish(phi_ts, own, recv, (to_x, to_d), (), tuple(q_shared))
        else:
            scale = scale_of(over_axis(keep[3 * nm:] + got[3 * nm:], "cluster"))
            scales.append(scale)
            p, resid, own = local_image(q, y, vec, phi_t, stack, (resid, scale, p, image), not last)
            resids.append(resid)
            early = ()
            if last:
                sol, final = directions(phi, phi_n, w, scales, resids, stacks)
            modal, far, near = finish(phi_ts, own, recv, (to_x, to_d), (scale, far, near), early)
        if not last:
            blocks = parity_blocks(modal)
            image, x_hi, x_lo = assemble(onehot_t, p, far, w)
            y = schur_apply(schur, (x_hi, x_lo))
    sums = over_mesh(modal[nm:])
    (image,) = assemble(onehot_t, p, far)
    scale = scale_of(sums)[0:1]
    return sol + scale * final, resid - scale * image


def solution(mesh):
    rows = P(BOTH, None)
    return jax.shard_map(
        program,
        mesh=mesh,
        in_specs=(rows, rows, rows, rows, P(BOTH), P(BOTH), rows, rows),
        out_specs=(rows, rows),
        check_vma=False,
    )
```

```python
import jax
import jax.numpy as jnp
from jax import lax
from jax.experimental import pallas as pl
from jax.experimental.pallas import tpu as pltpu
from jax.sharding import PartitionSpec as P


BOTH = ("cluster", "sub")
F32 = jnp.float32
BF16 = jnp.bfloat16
ITERS = 3
INTERPRET = False
SUMS = 8


def split2(x):
    hi = x.astype(BF16)
    return hi, (x - hi.astype(F32)).astype(BF16)


def split3(x):
    hi = x.astype(BF16)
    rest = x - hi.astype(F32)
    mid = rest.astype(BF16)
    return hi, mid, (rest - mid.astype(F32)).astype(BF16)


def mm(a, b):
    return jnp.dot(a, b, preferred_element_type=F32)


def mm3(a, b):
    return mm(jnp.concatenate([a[0], a[0]], 1), jnp.concatenate([b[0], b[1]], 0)) + mm(a[1], b[0])


def pick(onehot, parts):
    return mm(jnp.concatenate([onehot] * len(parts), 1), jnp.concatenate(parts, 0))


def shape(*dims, dtype=F32):
    return jax.ShapeDtypeStruct(dims, dtype)


def call(body, ins, outs, flops, scalars=(), scratch=(), mb=8, raw=(), after=()):
    moved = sum(a.size * a.dtype.itemsize for a in (*ins, *outs))
    lead = len(scalars) + len(raw) + len(ins)

    def run(*refs):
        body(*refs[:lead], *refs[lead + len(after):])

    anywhere = pl.BlockSpec(memory_space=pl.ANY)
    outside = pl.BlockSpec(memory_space=pltpu.HBM)
    on_chip = pl.BlockSpec(memory_space=pltpu.VMEM)
    return pl.pallas_call(
        run,
        in_specs=[pl.BlockSpec(memory_space=pltpu.SMEM)] * len(scalars) + [outside] * len(raw)
        + [on_chip] * len(ins) + [anywhere] * len(after),
        out_specs=[on_chip] * len(outs),
        out_shape=list(outs),
        scratch_shapes=list(scratch),
        cost_estimate=pl.CostEstimate(flops=int(flops), bytes_accessed=int(moved), transcendentals=0),
        compiler_params=pltpu.CompilerParams(vmem_limit_bytes=mb * 1024 * 1024),
        interpret=INTERPRET,
    )(*scalars, *[pltpu.with_memory_space_constraint(a, pltpu.HBM) for a in raw], *ins, *after)


def over_blocks(order, step, carry=0, unroll=False):
    b = block_of(order)
    if unroll:
        for k in range(0, order, b):
            carry = step(pl.ds(k, b), k, carry)
        return carry

    def one(k, carry):
        at = pl.multiple_of(k * b, b)
        return step(pl.ds(at, b), at, carry)

    return lax.fori_loop(0, order // b, one, carry)


def block_of(order):
    return 256 if order % 256 == 0 else order


def copy_rows(pairs, index_ref, base, half, order, masked):
    group = 8 if half % 8 == 0 else 1

    def step(j, _):
        rows = [index_ref[0, j * group + u] for u in range(group)]
        for source, out in pairs:
            values = [source[pl.ds(jnp.minimum(row, order - 1), 1), :] for row in rows]
            if masked:
                values = [jnp.where(row < order, value, 0.0) for row, value in zip(rows, values)]
            for u, value in enumerate(values):
                out[pl.ds(base + j * group + u, 1), :] = value
        return 0

    lax.fori_loop(0, half // group, step, 0)


def by_parity(me, work):
    even = lax.rem(me, 2) == 0
    pl.when(even)(lambda: work(1, 0))
    pl.when(jnp.logical_not(even))(lambda: work(0, 1))


def row_sides(me_ref, left_ref, right_ref):
    even = lax.rem(me_ref[0], 2) == 0
    left, right = left_ref[...], right_ref[...]
    return jnp.where(even, right, left), jnp.where(even, left, right)


def used_count(row, order):
    return jnp.sum(jnp.where(row < order, 1, 0))


def gather_load(me, left, right, load):
    half = left.shape[1]
    order, k = load.shape

    def body(me_ref, l_hbm, r_hbm, load_hbm, x_ref, d_ref, l_ref, r_ref, load_ref, sems):
        moves = [
            pltpu.make_async_copy(source, target, sems.at[i])
            for i, (source, target) in enumerate(((l_hbm, l_ref), (r_hbm, r_ref), (load_hbm, load_ref)))
        ]
        for move in moves:
            move.start()
        for move in moves:
            move.wait()
        rows = (l_ref, r_ref)

        def work(first, second):
            copy_rows([(load_ref, x_ref)], rows[first], 0, half, order, True)
            copy_rows([(load_ref, d_ref)], rows[second], 0, half, order, True)

        by_parity(me_ref[0], work)

    return call(
        body, [], [shape(half, k)] * 2, 0, [me], raw=[left, right, load],
        scratch=[pltpu.SMEM((1, half), jnp.int32)] * 2 + [pltpu.VMEM((order, k), F32), pltpu.SemaphoreType.DMA((3,))],
    )


def gather_shared(me, left, right, fields):
    half = left.shape[1]
    order = fields[0].shape[0]
    n = len(fields)

    def body(me_ref, l_ref, r_ref, *refs):
        rows = (l_ref, r_ref)
        pairs = list(zip(refs[:n], refs[n:]))

        def work(first, second):
            copy_rows(pairs, rows[first], 0, half, order, False)
            copy_rows(pairs, rows[second], half, half, order, False)

        by_parity(me_ref[0], work)

    outs = [shape(2 * half, f.shape[1]) for f in fields]
    return call(body, fields, outs, 2e9, [me, left, right], mb=4)


def gather_side(me, left, right, field, side):
    half = left.shape[1]
    order, k = field.shape

    def body(me_ref, l_ref, r_ref, field_ref, out_ref):
        rows = (l_ref, r_ref)
        by_parity(
            me_ref[0], lambda *sides: copy_rows([(field_ref, out_ref)], rows[sides[side]], 0, half, order, True)
        )

    return call(body, [field], [shape(half, k)], 1e9, [me, left, right], mb=4)[0]


def halves(me, inverse, after):
    nm, co = inverse.shape

    def body(me_ref, c_ref, same_ref, other_ref):
        par = lax.rem(me_ref[0], 2)
        for j in range(co // nm // 2):
            to = slice(j * nm, (j + 1) * nm)
            same_ref[:, to] = c_ref[:, pl.ds(pl.multiple_of((2 * j + par) * nm, nm), nm)]
            other_ref[:, to] = c_ref[:, pl.ds(pl.multiple_of((2 * j + 1 - par) * nm, nm), nm)]

    return call(body, [inverse], [shape(nm, co // 2)] * 2, 0, [me], after=after)


def prepare(me, live_rows, live_modes, left, right, schur, modes, load):
    order, nm = modes.shape
    half = left.shape[1]
    two = 2 * half
    pieces = half // nm
    tall = half + 8 * pieces
    b = block_of(order)
    k_load = load.shape[1]

    def body(me_ref, rows_ref, count_ref, s_hbm, modes_hbm, load_hbm, l_ref, r_ref,
             gt_ref, ph_ref, pl_ref, pth_ref, ptl_ref, vec_ref, x_ref, d_ref, tsh_ref, tsl_ref, m_ref,
             square_ref, modes_ref, load_ref, sems):
        def moves(r, columns, k):
            return [
                pltpu.make_async_copy(source, target.at[r], sems.at[i, k])
                for i, (source, target) in enumerate((
                    (s_hbm.at[r, columns], square_ref), (modes_hbm.at[r], modes_ref), (load_hbm.at[r], load_ref)
                ))
            ]

        for k in range(order // b):
            for move in moves(pl.ds(k * b, b), pl.ds(k * b, b), k):
                move.start()
        index = jnp.concatenate(row_sides(me_ref, l_ref, r_ref), axis=1)
        mask = jnp.where(lax.broadcasted_iota(jnp.int32, (1, nm), 1) < count_ref[0], 1.0, 0.0)
        eye = lax.broadcasted_iota(jnp.int32, (b, b), 0) == lax.broadcasted_iota(jnp.int32, (b, b), 1)
        lane = lax.broadcasted_iota(jnp.int32, (b, 128), 1)

        def step(r, start, carry):
            shared, weights, modal = carry
            for move in moves(r, r, start // b):
                move.wait()
            row_id = lax.broadcasted_iota(jnp.int32, (b, two), 0) + start
            found = jnp.where(index == row_id, 1.0, 0.0)
            gt = found.astype(BF16)
            gt_ref[r] = gt
            live = jnp.where(lax.broadcasted_iota(jnp.int32, (b, 1), 0) + start < rows_ref[0], 1.0, 0.0)
            share = live / (1.0 + jnp.sum(found, axis=1, keepdims=True))
            diag = jnp.sum(jnp.where(eye, square_ref[r], 0.0), axis=1, keepdims=True)
            sd = share / diag
            weights = weights + jnp.sum(found * sd, axis=0, keepdims=True)
            vec_ref[r] = jnp.where(lane == 0, live, sd)
            phi = share * (modes_ref[r] * mask)
            ph_ref[r], pl_ref[r] = split2(phi)
            parts = split3(phi.T)
            pth_ref[:, r], ptl_ref[:, r] = parts[:2]
            shared = shared + mm(jnp.concatenate(parts, 1), jnp.concatenate([gt] * 3, 0))
            return shared, weights, modal + mm3(parts[:2], split2(load_ref[r]))

        shared, weights, modal = over_blocks(
            order, step, (jnp.zeros((nm, two), F32), jnp.zeros((1, two), F32), jnp.zeros((nm, k_load), F32))
        )
        m_ref[:nm] = modal
        m_ref[nm:] = jnp.zeros((SUMS, k_load), F32)
        tsh_ref[...], tsl_ref[...] = split2(shared)
        back = shared.T
        for i, ref in enumerate((x_ref, d_ref)):
            ref[:half] = back[i * half:(i + 1) * half]
            for t in range(pieces):
                at = i * half + t * nm
                ref[half + 8 * t:half + 8 * t + 8] = jnp.broadcast_to(weights[:, at:at + nm], (8, nm))

    half_type = dict(dtype=BF16)
    return call(
        body, [left, right],
        [shape(order, two, **half_type), shape(order, nm, **half_type), shape(order, nm, **half_type),
         shape(nm, order, **half_type), shape(nm, order, **half_type), shape(order, 128),
         shape(tall, nm), shape(tall, nm), shape(nm, two, **half_type), shape(nm, two, **half_type),
         shape(nm + SUMS, k_load)],
        6 * two * order * nm, [me, live_rows, live_modes], raw=[schur, modes, load], mb=14,
        scratch=[pltpu.VMEM((order, b), F32), pltpu.VMEM((order, nm), F32), pltpu.VMEM((order, k_load), F32),
                 pltpu.SemaphoreType.DMA((3, order // b))],
    )


def extend(onehot_t, vec, load, recv, phi_recv):
    order, two = onehot_t.shape
    half = two // 2
    k = load.shape[1]
    nm = phi_recv[0].shape[1]
    pieces = half // nm

    def body(gt_ref, vec_ref, f_ref, rx_ref, rd_ref, px_ref, pd_ref, r_ref, w_ref, nh_ref, nl_ref):
        field = [jnp.concatenate(p, 0) for p in zip(split2(rx_ref[...]), split2(rd_ref[...]))]
        weights = jnp.concatenate(
            [ref[half + 8 * t:half + 8 * t + 1] for ref in (px_ref, pd_ref) for t in range(pieces)], axis=1
        )
        modes = [jnp.concatenate(split2(ref[:half]), 0) for ref in (px_ref, pd_ref)]

        def step(r, _, carry):
            gt = gt_ref[r]
            w = vec_ref[r, 1:2] + jnp.sum(gt.astype(F32) * weights, axis=1, keepdims=True)
            w_ref[r] = jnp.broadcast_to(w, (w.shape[0], 128))
            r_ref[r] = vec_ref[r, 0:1] * f_ref[r] + pick(gt, field)
            for i in range(2):
                side = gt[:, i * half:(i + 1) * half]
                part = mm(jnp.concatenate([side, side], 1), modes[i])
                nh_ref[r, i * nm:(i + 1) * nm], nl_ref[r, i * nm:(i + 1) * nm] = split2(part)
            return carry

        over_blocks(order, step)

    return call(
        body, [onehot_t, vec, load, *recv, *phi_recv],
        [shape(order, k), shape(order, 128)] + [shape(order, 2 * nm, dtype=BF16)] * 2,
        2 * order * two * (3 * k + 2 * nm), mb=12,
    )


def schur_modes(schur, modes, unroll):
    order, n = modes[0].shape

    def body(s_ref, h_ref, l_ref, q_ref):
        rhs = (h_ref[...], l_ref[...])

        def block(r, _, carry):
            q_ref[r] = mm3(split2(s_ref[r]), rhs)
            return carry

        over_blocks(order, block, unroll=unroll)

    return call(body, [schur, *modes], [shape(order, n)], 6 * order * order * n, mb=10)[0]


def schur_apply(schur, x):
    order, k = x[0].shape

    def body(s_ref, xh_ref, xl_ref, y_ref):
        x = (xh_ref[...], xl_ref[...])

        def block(r, _, carry):
            y_ref[r] = mm3(split2(s_ref[r]), x)
            return carry

        over_blocks(order, block, unroll=True)

    return call(body, [schur, *x], [shape(order, k)], 6 * order * order * k, mb=10)[0]


def coarse(me, inverses, modal, after):
    nm, co = inverses[0].shape
    _, k = modal[0].shape
    n = len(modal)
    ordered = direct(2 * n)

    def body(me_ref, own_ref, x_ref, d_ref, z_ref, *rest):
        send_ref, keep_ref, d_out, z_out, xh, xl = rest[n:]
        pos = me_ref[0] // 2
        sums = jnp.zeros((SUMS, k), F32)
        for d in range(n):
            at = pl.ds(pl.multiple_of(((pos ^ d) if ordered else d) * nm, nm), nm)
            xh[at], xl[at] = split2(rest[d][:nm])
            sums = sums + rest[d][nm:]
        a = split2(jnp.concatenate([own_ref[...], x_ref[...], d_ref[...], z_ref[...]], 0))
        part = mm3(a, (xh[...], xl[...]))
        keep_ref[:3 * nm] = part[:3 * nm]
        keep_ref[3 * nm:] = sums
        send_ref[:nm] = part[nm:2 * nm]
        send_ref[nm:2 * nm] = part[:nm]
        send_ref[2 * nm:3 * nm] = part[3 * nm:]
        send_ref[3 * nm:] = sums
        d_out[...] = part[2 * nm:3 * nm]
        z_out[...] = part[3 * nm:]

    return call(
        body, [*inverses, *modal], [shape(3 * nm + SUMS, k)] * 2 + [shape(nm, k)] * 2,
        24 * nm * co * k, [me], scratch=[pltpu.VMEM((co, k), BF16)] * 2, mb=12, after=after,
    )


def whole_stack(me, last_sub, keep, recv, edges, out):
    nm = edges[0].shape[0]
    at_edge = jnp.logical_or(me == 0, me == last_sub)
    total = keep[:3 * nm] + recv[:3 * nm]
    out[:2 * nm] = total[:2 * nm]
    out[2 * nm:] = jnp.where(at_edge, edges[0][...] + edges[1][...], total[2 * nm:])


def first_direction(me, last_sub, keep, recv, edges, phi, phi_n, w, resid):
    order, nm = phi[0].shape
    k = resid.shape[1]

    def body(me_ref, keep_ref, recv_ref, e1_ref, e2_ref, h_ref, l_ref, nh_ref, nl_ref, w_ref, r_ref,
             st_ref, xh_ref, xl_ref):
        whole_stack(me_ref[0], last_sub, keep_ref, recv_ref, (e1_ref, e2_ref), st_ref)
        c = split2(st_ref[...])

        def step(r, _, carry):
            p = (jnp.concatenate([h_ref[r], nh_ref[r]], 1), jnp.concatenate([l_ref[r], nl_ref[r]], 1))
            xh_ref[r], xl_ref[r] = split2(mm3(p, c) + w_ref[r, 0:1] * r_ref[r])
            return carry

        over_blocks(order, step, unroll=True)

    return call(
        body, [keep, recv, *edges, *phi, *phi_n, w, resid],
        [shape(3 * nm, k)] + [shape(order, k, dtype=BF16)] * 2, 18 * order * nm * k, [me], mb=10,
    )


def first_image(y, vec, phi_t, resid):
    order, k = y.shape
    nm = phi_t[0].shape[0]

    def body(y_ref, vec_ref, th_ref, tl_ref, r_ref, p_ref, m_ref):
        def step(at, _, carry):
            num, den, modal = carry
            p = vec_ref[at, 0:1] * y_ref[at]
            p_ref[at] = p
            num = num + jnp.sum(r_ref[at] * p, axis=0, keepdims=True)
            den = den + jnp.sum(p * p, axis=0, keepdims=True)
            return num, den, modal + mm3((th_ref[:, at], tl_ref[:, at]), split2(p))

        zero = jnp.zeros((1, k), F32)
        num, den, modal = over_blocks(order, step, (zero, zero, jnp.zeros((nm, k), F32)))
        row = lax.broadcasted_iota(jnp.int32, (SUMS, k), 0)
        m_ref[:nm] = modal
        m_ref[nm:] = jnp.where(row == 0, num, jnp.where(row == 1, den, 0.0))

    return call(body, [y, vec, *phi_t, resid], [shape(order, k), shape(nm + SUMS, k)], 6 * nm * order * k, mb=8)


def shared_image(me, last_sub, left, right, order, q_shared, y_shared, keep, recv, edges):
    two = y_shared.shape[0]
    half = two // 2
    nm, k = edges[0].shape
    n = 3 * nm

    def body(me_ref, lv_ref, rv_ref, qo_ref, qn_ref, y_ref, keep_ref, recv_ref, e1_ref, e2_ref, x_ref, d_ref, st_ref):
        rows = row_sides(me_ref, lv_ref, rv_ref)
        whole_stack(me_ref[0], last_sub, keep_ref, recv_ref, (e1_ref, e2_ref), st_ref)
        c = split2(st_ref[...])
        for i, ref in enumerate((x_ref, d_ref)):
            at = slice(i * half, (i + 1) * half)
            found = y_ref[at] + mm3(split2(jnp.concatenate([qo_ref[at], qn_ref[at]], 1)), c)
            slot = lax.broadcasted_iota(jnp.int32, (half, k), 0)
            ref[...] = jnp.where(slot < used_count(rows[i], order), found, 0.0)

    return call(
        body, [left, right, *q_shared, y_shared, keep, recv, *edges],
        [shape(half, k)] * 2 + [shape(3 * nm, k)], 6 * two * n * k, [me], mb=10,
    )


def local_image(q, y, vec, phi_t, stack, chain, restrict):
    order = y.shape[0]
    n, k = stack.shape
    nm = phi_t[0].shape[0]

    def body(qo_ref, qn_ref, y_ref, vec_ref, th_ref, tl_ref, st_ref, *refs):
        ins, outs = refs[:len(chain)], list(refs[len(chain):])
        c = split2(st_ref[...])
        p_ref = outs.pop(0)
        r_ref = outs.pop(0)

        def step(at, _, carry):
            num, den, modal = carry
            p = vec_ref[at, 0:1] * (y_ref[at] + mm3(split2(jnp.concatenate([qo_ref[at], qn_ref[at]], 1)), c))
            scale = ins[1][0:1]
            p = ins[2][at] - scale * p
            r = ins[0][at] - scale * ins[3][at]
            r_ref[at] = r
            p_ref[at] = p
            num = num + jnp.sum(r * p, axis=0, keepdims=True)
            den = den + jnp.sum(p * p, axis=0, keepdims=True)
            if restrict:
                modal = modal + mm3((th_ref[:, at], tl_ref[:, at]), split2(p))
            return num, den, modal

        zero = jnp.zeros((1, k), F32)
        num, den, modal = over_blocks(order, step, (zero, zero, jnp.zeros((nm, k), F32)))
        row = lax.broadcasted_iota(jnp.int32, (SUMS, k), 0)
        m_ref = outs.pop(0)
        m_ref[:nm] = modal
        m_ref[nm:] = jnp.where(row == 0, num, jnp.where(row == 1, den, 0.0))

    outs = [shape(order, k)] * 2 + [shape(nm + SUMS, k)]
    return call(
        body, [*q, y, vec, *phi_t, stack, *chain], outs,
        6 * order * n * k + 6 * nm * order * k, mb=12,
    )


def finish(phi_ts, own, recv, sent=(), chain=(), after=()):
    nm, two = phi_ts[0].shape
    k = own.shape[1]
    plain = len(sent) == 0

    def body(h_ref, l_ref, m_ref, *refs):
        ins, outs = refs[:2 + len(sent) + len(chain)], refs[2 + len(sent) + len(chain):]
        got = jnp.concatenate([ins[0][...], ins[1][...]], 0)
        cross = jnp.zeros((1, k), F32)
        if not plain:
            put = jnp.concatenate([ins[2][...], ins[3][...]], 0)
            if chain:
                scale = ins[4][0:1]
                got = ins[5][...] - scale * got
                put = ins[6][...] - scale * put
            outs[1][...] = got
            outs[2][...] = put
            cross = jnp.sum(got * put, axis=0, keepdims=True)
        outs[0][:nm] = m_ref[:nm] + mm3((h_ref[...], l_ref[...]), split2(got))
        row = lax.broadcasted_iota(jnp.int32, (SUMS, k), 0)
        base = m_ref[nm:] if not plain else jnp.zeros((SUMS, k), F32)
        outs[0][nm:] = base + jnp.where(row == 1, cross, 0.0)

    outs = [shape(nm + SUMS, k)] + ([] if plain else [shape(two, k)] * 2)
    return call(body, [*phi_ts, own, *recv, *sent, *chain], outs, 6 * nm * two * k, mb=10, after=after)


def assemble(onehot_t, p, got, w=None):
    order, two = onehot_t.shape
    k = p.shape[1]

    def body(gt_ref, p_ref, g_ref, *refs):
        parts = jnp.concatenate(split2(g_ref[...]), 0)

        def step(r, _, carry):
            gt = gt_ref[r]
            new = p_ref[r] + mm(jnp.concatenate([gt, gt], 1), parts)
            if w is None:
                refs[0][r] = new
            else:
                w_ref, i_ref, xh_ref, xl_ref = refs
                i_ref[r] = new
                xh_ref[r], xl_ref[r] = split2(w_ref[r, 0:1] * new)
            return carry

        over_blocks(order, step, unroll=True)

    ins = [onehot_t, p, got] + ([] if w is None else [w])
    outs = [shape(order, k)] + ([] if w is None else [shape(order, k, dtype=BF16)] * 2)
    return call(body, ins, outs, 4 * order * two * k, mb=10)


def directions(phi, phi_n, w, scales, resids, stacks):
    order, _ = phi[0].shape
    n, k = stacks[0].shape

    def body(h_ref, l_ref, nh_ref, nl_ref, w_ref, a0_ref, a1_ref, r0_ref, r1_ref, r2_ref,
             c0_ref, e0_ref, e1_ref, sol_ref, dir_ref):
        s0, s1 = a0_ref[0:1], a1_ref[0:1]
        c0 = c0_ref[...]
        c1 = c0 - s0 * e0_ref[...]
        first = s0 * c0 + s1 * c1
        c = split2(jnp.concatenate([first, c1 - s1 * e1_ref[...]], 1))

        def step(r, _, carry):
            p = (jnp.concatenate([h_ref[r], nh_ref[r]], 1), jnp.concatenate([l_ref[r], nl_ref[r]], 1))
            both = mm3(p, c)
            wc = w_ref[r, 0:1]
            sol_ref[r] = both[:, :k] + wc * (s0 * r0_ref[r] + s1 * r1_ref[r])
            dir_ref[r] = both[:, k:] + wc * r2_ref[r]
            return carry

        over_blocks(order, step)

    return call(
        body, [*phi, *phi_n, w, *scales, *resids, *stacks], [shape(order, k)] * 2,
        12 * order * n * k, mb=12,
    )


def swap_x(value):
    n = lax.axis_size("sub")
    return lax.ppermute(value, "sub", [(i, i ^ 1) for i in range(n)])


def swap_d(value):
    n = lax.axis_size(BOTH)
    pairs = [(i, i + 1) for i in range(1, n - 1, 2)]
    return lax.ppermute(value, BOTH, pairs + [(b, a) for a, b in pairs])


def coarse_rows(me, inverse, after):
    n = lax.axis_size("sub")
    same, other = halves(me, inverse, after)
    at_z = lax.ppermute(same, "sub", [(i, (i - 2) % n if i % 2 == 0 else (i + 2) % n) for i in range(n)])
    return same, at_z, other


def coarse_partners(other):
    n = lax.axis_size("sub")
    ring = [((i + 1) % n, (i + 2) % n) for i in range(0, n, 2)]
    return swap_x(other), lax.ppermute(other, "sub", ring + [(b, a) for a, b in ring])


def direct(n):
    return n & (n - 1) == 0 and n <= 8


def parity_blocks(modal):
    n = lax.axis_size("sub")
    if not direct(n):
        groups = [list(range(p, n, 2)) for p in range(2)]
        every = lax.all_gather(modal, "sub", axis=0, axis_index_groups=groups)
        return [every[d] for d in range(n // 2)]
    return [modal] + [
        lax.ppermute(modal, "sub", [(i, i ^ (2 * d)) for i in range(n)]) for d in range(1, n // 2)
    ]


def over_axis(value, axis):
    n = lax.axis_size(axis)
    if n & (n - 1):
        return lax.psum(value, axis)
    step = 1
    while step < n:
        value = value + lax.ppermute(value, axis, [(i, i ^ step) for i in range(n)])
        step *= 2
    return value


def over_mesh(value):
    m, n = lax.axis_size("cluster"), lax.axis_size("sub")
    if m < 4 or n < 2 or m & (m - 1) or n & (n - 1):
        return over_axis(over_axis(value, "cluster"), "sub")
    value = value + lax.ppermute(value, "cluster", [(i, i ^ 1) for i in range(m)])
    here = [(c, s) for c in range(m) for s in range(n)]
    round_of = [(2, 0), (0, 1), (2, 1)]
    got = [
        lax.ppermute(value, BOTH, [(c * n + s, (c ^ up) * n + (s ^ along)) for c, s in here])
        for up, along in round_of
    ]
    value = (value + got[0]) + (got[1] + got[2])
    for step in [4 << i for i in range(8) if 4 << i < m]:
        value = value + lax.ppermute(value, "cluster", [(i, i ^ step) for i in range(m)])
    for step in [2 << i for i in range(8) if 2 << i < n]:
        value = value + lax.ppermute(value, "sub", [(i, i ^ step) for i in range(n)])
    return value


def edge_blocks(block, partner):
    n, m = lax.axis_size("sub"), lax.axis_size("cluster")
    out = []
    for value, shift in ((block, 0), (partner, 1)):
        up = [(n * c + shift, n * (c + 1)) for c in range(m - 1)]
        down = [(n * (c + 1) + n - 1 - shift, n * c + n - 1) for c in range(m - 1)]
        out.append(lax.ppermute(value, BOTH, up + down))
    return out


def scale_of(sums):
    value = sums[0:1] / (sums[1:2] + 1e-06)
    return jnp.broadcast_to(value, (8, value.shape[1]))


def program(load, schur, modes, coarse_inverse, interface_rows, mode_count, left_rows, right_rows):
    nm = modes.shape[1]
    n_sub = lax.axis_size("sub")
    me = lax.axis_index("sub").astype(jnp.int32).reshape(1)

    to_x, to_d = gather_load(me, left_rows, right_rows, load)
    recv = swap_x(to_x), swap_d(to_d)
    onehot_t, p_hi, p_lo, pt_hi, pt_lo, vec, phi_x, phi_d, ts_hi, ts_lo, own = prepare(
        me, interface_rows, mode_count, left_rows, right_rows, schur, modes, load
    )
    phi, phi_t, phi_ts = (p_hi, p_lo), (pt_hi, pt_lo), (ts_hi, ts_lo)
    rows_own, rows_z, other = coarse_rows(me, coarse_inverse, (own,))
    q_own = schur_modes(schur, phi, True)
    (modal,) = finish(phi_ts, own, recv, after=(q_own,))
    blocks = parity_blocks(modal)
    other, _ = lax.optimization_barrier((other, modal))
    inverses = (rows_own, *coarse_partners(other), rows_z)
    phi_recv = swap_x(phi_x), swap_d(phi_d)
    resid, w, n_hi, n_lo = extend(onehot_t, vec, load, recv, phi_recv)
    phi_n = (n_hi, n_lo)

    scales, resids, stacks = [], [resid], []
    for iteration in range(ITERS):
        first, last = iteration == 0, iteration == ITERS - 1
        send, keep, end_d, end_z = coarse(me, inverses, blocks, () if first else (y,))
        got = swap_x(send)
        edges = edge_blocks(end_d, end_z)
        if first:
            stack, x_hi, x_lo = first_direction(me, n_sub - 1, keep, got, edges, phi, phi_n, w, resid)
            y = schur_apply(schur, (x_hi, x_lo))
            to_x = gather_side(me, left_rows, right_rows, y, 0)
            to_d = gather_side(me, left_rows, right_rows, y, 1)
        else:
            (y_shared,) = gather_shared(me, left_rows, right_rows, [y])
            to_x, to_d, stack = shared_image(
                me, n_sub - 1, left_rows, right_rows, schur.shape[0], q_shared, y_shared, keep, got, edges
            )
        stacks.append(stack)
        from_x = swap_x(to_x)
        recv = from_x, swap_d(to_d)
        if first:
            p, own = first_image(y, vec, phi_t, resid)
            q = (q_own, schur_modes(schur, phi_n, False))
            q_shared = gather_shared(me, left_rows, right_rows, list(q))
            modal, far, near = finish(phi_ts, own, recv, (to_x, to_d), (), tuple(q_shared))
        else:
            scale = scale_of(over_axis(keep[3 * nm:] + got[3 * nm:], "cluster"))
            scales.append(scale)
            p, resid, own = local_image(q, y, vec, phi_t, stack, (resid, scale, p, image), not last)
            resids.append(resid)
            early = ()
            if last:
                sol, final = directions(phi, phi_n, w, scales, resids, stacks)
            modal, far, near = finish(phi_ts, own, recv, (to_x, to_d), (scale, far, near), early)
        if not last:
            blocks = parity_blocks(modal)
            image, x_hi, x_lo = assemble(onehot_t, p, far, w)
            y = schur_apply(schur, (x_hi, x_lo))
    sums = over_mesh(modal[nm:])
    (image,) = assemble(onehot_t, p, far)
    scale = scale_of(sums)[0:1]
    return sol + scale * final, resid - scale * image


def solution(mesh):
    rows = P(BOTH, None)
    return jax.shard_map(
        program,
        mesh=mesh,
        in_specs=(rows, rows, rows, rows, P(BOTH), P(BOTH), rows, rows),
        out_specs=(rows, rows),
        check_vma=False,
    )
```
